256 devices in a mesh: gx: 4 (over x), gy: 8 (over y, z_lo), gz: 8 (over z_hi, core).
Axes of the slice: x: 4, y: 4, z: 8 (z_hi: 4, z_lo: 2; z = z_hi * 2 + z_lo), core: 2. Of those that a mesh axis runs over, the one named last changes fastest.
Arguments:
- features: bfloat16 [4, 8, 16, 128, 128], P('gx', 'gy', 'gz'), may hold values from -6 to 6
- positions: int32 [3, 4, 8, 16, 128], P(None, 'gx', 'gy', 'gz'), may hold values from 0 to 63
- wavevectors: int32 [3, 1024], replicated, may hold values from -6 to 6
- radial_mix: bfloat16 [768, 128], replicated, may hold values from -0.0546875 to 0.0546875
- charge_weight: bfloat16 [128, 128], replicated, may hold values from -0.5 to 0.5
- filters: float32 [1024, 128], replicated, may hold values from 0.01 to 0.1
- mix_weight: float32 [128, 128], replicated, may hold values from -0.5 to 0.5
- norm_gain: float32 [128], replicated, may hold values from 0.1 to 1.9
- up_weight: bfloat16 [128, 256], replicated, may hold values from -0.5 to 0.5
- down_weight: bfloat16 [256, 128], replicated, may hold values from -0.375 to 0.375
Outputs:
- updated: bfloat16 [4, 8, 16, 128, 128], P('gx', 'gy', 'gz')
The draws below stay inside these ranges and needn't reach their ends.
All inputs are finite; a program needn't handle non-finite values.
Results may differ from the reference program's by a relative error of at most 0.006.
Values may be sent and summed in bfloat16 or wider, within the bound.
A program may use at most 64 MiB of HBM per device.

```python
import math
import jax
import jax.numpy as jnp
from jax import lax

D = 128
HID = 256
NRBF = 6
TILE = 128
K = 1024
GRID = 64
NTX = 4
NTY = 8
NTZ = 16


def touch_ends(values, stream_key, smallest, largest):
    spot = [jax.random.randint(jax.random.fold_in(stream_key, axis), (), 0, length) for axis, length in enumerate(values.shape)]
    longest = values.shape.index(max(values.shape))
    beside = spot[:longest] + [(spot[longest] + 1) % values.shape[longest]] + spot[longest + 1:]
    return values.at[tuple(spot)].set(smallest).at[tuple(beside)].set(largest)


def shard_levels(rng, dims, pieces, low, largest):
    level, own = 1.0, jax.random.fold_in(rng, 6)
    for axis_at, shards_of in pieces:
        steps = jnp.exp(jax.random.uniform(jax.random.fold_in(own, axis_at), (shards_of,), jnp.float32, low / len(pieces), largest / len(pieces)))
        level = level * jnp.repeat(steps, dims[axis_at] // shards_of).reshape([-1 if axis == axis_at else 1 for axis in range(len(dims))])
    return level


def scatter_about(own_key, shape, width, reach, pieces=(), kind=jnp.bfloat16):
    drawn = width * jax.random.normal(own_key, shape, jnp.float32)
    if pieces:
        drawn = drawn * shard_levels(own_key, shape, pieces, -0.22, 0.18)
    return jnp.clip(drawn, -reach, reach).astype(kind)


def setup_inputs(seed: int = 0) -> dict:
    seeds = jax.random.split(jax.random.key(seed), 11)
    return {
        "features": scatter_about(seeds[0], (NTX, NTY, NTZ, TILE, D), 1.0, 6.0, ((0, 4), (1, 8), (2, 8))),
        "positions": touch_ends(jax.random.randint(seeds[1], (3, NTX, NTY, NTZ, TILE), 0, GRID), jax.random.fold_in(seeds[1], 1), 0, GRID - 1).astype(jnp.int32),
        "wavevectors": touch_ends(jax.random.randint(seeds[2], (3, K), -6, 7), jax.random.fold_in(seeds[2], 1), -6, 6).astype(jnp.int32),
        "radial_mix": scatter_about(seeds[3], (NRBF * D, D), (16 * NRBF * D) ** -0.5, 0.0546875),
        "charge_weight": scatter_about(seeds[4], (D, D), D ** -0.5, 0.5),
        "filters": jnp.clip(jnp.exp(jax.random.uniform(seeds[5], (K, D), jnp.float32, math.log(0.01), math.log(0.1))), 0.01, 0.1),
        "mix_weight": scatter_about(seeds[6], (D, D), D ** -0.5, 0.5, (), jnp.float32),
        "norm_gain": jnp.clip(1.0 + 0.18 * jax.random.normal(seeds[7], (D,), jnp.float32), 0.1, 1.9),
        "up_weight": scatter_about(seeds[8], (D, HID), D ** -0.5, 0.5),
        "down_weight": scatter_about(seeds[9], (HID, D), HID ** -0.5, 0.375),
    }


SHARP = 18.0
TWO_PI = 2.0 * math.pi
EPS = 1e-06
CONTRACT_FIRST = (((0,), (0,)), ((), ()))

def radial_basis(center, nearby_pos):
    tile_size = center.shape[1]
    offsets = jnp.stack([lax.broadcasted_iota(jnp.int32, (3, 3, 3, 1), component) for component in range(3)]) - 1
    coords = (nearby_pos + offsets * GRID).reshape(3, 27 * tile_size)
    displace = coords[:, None, :] - center[:, :, None]
    square = lax.optimization_barrier(jnp.sum(displace * displace, axis=0))
    scaled_dist = jnp.sqrt(square.astype(jnp.float32)) / GRID
    inside = (square > 0) & (square < GRID * GRID)
    envelope = jnp.where(inside, (1.0 - scaled_dist * scaled_dist) ** 2, 0.0)
    centres = (jnp.arange(NRBF, dtype=jnp.float32) + 0.5) / NRBF
    radial = jnp.exp(-SHARP * (scaled_dist[:, None, :] - centres[None, :, None]) ** 2) * envelope[:, None, :]
    return radial.astype(jnp.bfloat16)

def tile_message(center, nearby_pos, neighbour, radial_mix):
    tile_size = center.shape[1]
    radial = radial_basis(center, nearby_pos)
    pooled = jnp.einsum('irj,jd->ird', radial.astype(jnp.float32), neighbour.astype(jnp.float32))
    pooled = pooled.astype(jnp.bfloat16).reshape(tile_size, -1)
    return jnp.dot(pooled, radial_mix, preferred_element_type=jnp.float32)

def phase_tables(wavevectors, coords, lengths):
    fraction = jnp.zeros((wavevectors.shape[1], coords.shape[1]), jnp.float32)
    for component in range(3):
        product = jnp.mod(wavevectors[component][:, None] * coords[component][None, :], lengths[component])
        fraction = fraction + product.astype(jnp.float32) / lengths[component]
    phase_angle = TWO_PI * fraction
    return (jnp.cos(phase_angle).astype(jnp.bfloat16), jnp.sin(phase_angle).astype(jnp.bfloat16))

def reference(features, positions, wavevectors, radial_mix, charge_weight, filters, mix_weight, norm_gain, up_weight, down_weight):
    count_x, count_y, count_z, tile_size, feat_width = features.shape
    pad_feat = jnp.pad(features, ((1, 1), (1, 1), (1, 1), (0, 0), (0, 0)), mode='wrap')
    pad_pos = jnp.pad(positions, ((0, 0), (1, 1), (1, 1), (1, 1), (0, 0)), mode='wrap')
    anchor = jnp.zeros((), jnp.int32)

    def one_tile(flat_index):
        tile_x = (flat_index // (count_y * count_z)).astype(jnp.int32)
        tile_y = (flat_index // count_z % count_y).astype(jnp.int32)
        tile_z = (flat_index % count_z).astype(jnp.int32)
        neighbour = lax.dynamic_slice(pad_feat, (tile_x, tile_y, tile_z, anchor, anchor), (3, 3, 3, tile_size, feat_width))
        nearby_pos = lax.dynamic_slice(pad_pos, (anchor, tile_x, tile_y, tile_z, anchor), (3, 3, 3, 3, tile_size))
        center = lax.dynamic_slice(positions, (anchor, tile_x, tile_y, tile_z, anchor), (3, 1, 1, 1, tile_size)).reshape(3, tile_size)
        return tile_message(center, nearby_pos, neighbour.reshape(27 * tile_size, feat_width), radial_mix)
    message = lax.map(one_tile, jnp.arange(count_x * count_y * count_z, dtype=jnp.int32))
    message = message.reshape(count_x, count_y, count_z, tile_size, feat_width)
    lengths = (count_x * GRID, count_y * GRID, count_z * GRID)
    charges = jnp.dot(features.reshape(-1, feat_width), charge_weight, preferred_element_type=jnp.float32)
    charges = charges.astype(jnp.bfloat16).reshape(count_x * count_y, count_z * tile_size, feat_width)

    def row_coords(row_index):
        tile_x = (row_index // count_y).astype(jnp.int32)
        tile_y = (row_index % count_y).astype(jnp.int32)
        local_pos = lax.dynamic_slice(positions, (anchor, tile_x, tile_y, anchor, anchor), (3, 1, 1, count_z, tile_size)).reshape(3, count_z, tile_size)
        zeros_int = jnp.zeros((count_z, tile_size), jnp.int32)
        tile_coord = jnp.stack([tile_x + zeros_int, tile_y + zeros_int, lax.broadcasted_iota(jnp.int32, (count_z, tile_size), 0)])
        return (tile_coord * GRID + local_pos).reshape(3, count_z * tile_size)

    def add_row(totals, row_index):
        cos_table, sin_table = phase_tables(wavevectors, row_coords(row_index), lengths)
        row_charges = charges[row_index]
        return ((totals[0] + jnp.dot(cos_table, row_charges, preferred_element_type=jnp.float32), totals[1] + jnp.dot(sin_table, row_charges, preferred_element_type=jnp.float32)), None)
    start_sums = (jnp.zeros((wavevectors.shape[1], feat_width), jnp.float32), jnp.zeros((wavevectors.shape[1], feat_width), jnp.float32))
    sums, unused = lax.scan(add_row, start_sums, jnp.arange(count_x * count_y, dtype=jnp.int32))
    scale = 1.0 / math.sqrt(count_x * count_y * count_z * tile_size)
    filtered_cos = jnp.dot(filters * (sums[0] * scale), mix_weight, precision=lax.Precision.HIGHEST).astype(jnp.bfloat16)
    filtered_sin = jnp.dot(filters * (sums[1] * scale), mix_weight, precision=lax.Precision.HIGHEST).astype(jnp.bfloat16)

    def row_long(row_index):
        cos_table, sin_table = phase_tables(wavevectors, row_coords(row_index), lengths)
        result = lax.dot_general(cos_table.astype(jnp.float32), filtered_cos.astype(jnp.float32), CONTRACT_FIRST)
        return result + lax.dot_general(sin_table.astype(jnp.float32), filtered_sin.astype(jnp.float32), CONTRACT_FIRST)
    longrange = lax.map(row_long, jnp.arange(count_x * count_y, dtype=jnp.int32))
    longrange = longrange.reshape(count_x, count_y, count_z, tile_size, feat_width)
    summed = features.astype(jnp.float32) + message + longrange
    flat_sum = summed.reshape(-1, feat_width)
    normed = flat_sum * lax.rsqrt(lax.optimization_barrier(jnp.mean(flat_sum * flat_sum, axis=-1, keepdims=True)) + EPS) * norm_gain
    hidden = jax.nn.silu(jnp.dot(normed.astype(jnp.bfloat16), up_weight, preferred_element_type=jnp.float32)).astype(jnp.bfloat16)
    updated = flat_sum + jnp.dot(hidden, down_weight, preferred_element_type=jnp.float32)
    return updated.reshape(features.shape).astype(jnp.bfloat16)
```

```python
import functools
import math

import jax
import jax.numpy as jnp
from jax import lax
from jax.experimental import pallas as pl
from jax.experimental.pallas import tpu as pltpu
from jax.sharding import PartitionSpec as P

MESH = pl.DeviceIdType.MESH
F32, BF16 = jnp.float32, jnp.bfloat16
NRBF = 6
GRID = 64
TILE = 128
D = 128
K = 1024
EPS = 1e-06
NX, NY, NZ = 4, 4, 8
LOG2E = 1.4426950408889634
SIN = (
    6.283182818518357,
    -41.341421396050286,
    81.5961838134782,
    -76.58009997779837,
    41.20539265997673,
    -12.271259128462068,
)
FIRST = (((0,), (0,)), ((), ()))


def rows16(values, width):
    row = lax.broadcasted_iota(jnp.int32, (16, width), 0)
    out = jnp.zeros((16, width), F32)
    for at, value in enumerate(values):
        out = jnp.where(row == at, value, out)
    return out.astype(BF16)


def sine_of_cycles(cycles):
    f = cycles - jnp.round(cycles)
    u = f * f
    acc = SIN[5]
    for c in SIN[4::-1]:
        acc = acc * u + c
    return acc * f


def lanes(tiles):
    return jnp.concatenate(tiles, axis=1)


def kernel(
    feat_hbm,
    pos_hbm,
    wave_ref,
    rmix_ref,
    cw_ref,
    filt_hbm,
    mix_ref,
    gain_ref,
    up_ref,
    down_ref,
    out_ref,
    halo,
    halo_pos,
    pair,
    pair_pos,
    tab_k,
    tab_i,
    rs_send,
    rs_recv,
    rz_send,
    rz_recv,
    filt,
    gz_send,
    gz_recv,
    ga_send,
    ga_recv,
    ls_send,
    ls_recv,
    kv,
    charge,
    q2,
    rad0,
    rad1,
    pool,
    far,
    load_sem,
    filt_sem,
    pair_sem,
    hz_sem,
    hy_sem,
    hx_sem,
    hc_sem,
    coll_sem,
):
    gx, gy, gz = lax.axis_index("gx"), lax.axis_index("gy"), lax.axis_index("gz")
    x, y, zl, zh, c = gx, gy // 2, gy % 2, gz // 2, gz % 2
    z = zh * 2 + zl
    q = x * NY + y

    def at(gx_, gy_, gz_):
        return {"gx": gx_, "gy": gy_, "gz": gz_}

    def xy_peer(i):
        return at(i // NY, (i % NY) * 2 + zl, gz)

    def z_peer(i):
        return at(gx, y * 2 + i % 2, (i // 2) * 2 + c)

    partner = at(gx, gy, gz + 1 - 2 * c)
    cross = at(gx, gy, (gz + 2 * c + 7) % 8)
    gy_up, gy_down = at(gx, (gy + 1) % 8, gz), at(gx, (gy + 7) % 8, gz)
    gx_up, gx_down = at((gx + 1) % 4, gy, gz), at((gx + 3) % 4, gy, gz)
    far_y = at(gx, (gy + 2 * zl + 7) % 8, gz)

    loads = [
        pltpu.make_async_copy(feat_hbm, halo.at[4, pl.ds(1, 2)], load_sem.at[0]),
        pltpu.make_async_copy(pos_hbm, halo_pos.at[4, pl.ds(1, 2)], load_sem.at[1]),
    ]
    for load in loads:
        load.start()
    mine = pl.multiple_of(q * 64 + z * 8, 8)
    filt_load = pltpu.make_async_copy(filt_hbm.at[pl.ds(mine, 8)], filt, filt_sem)
    filt_load.start()

    barrier = pltpu.get_barrier_semaphore()

    def greet(peer):
        pl.semaphore_signal(barrier, inc=1, device_id=peer, device_id_type=MESH)

    greet(partner)
    greet(cross)
    greet(far_y)

    def greet_xy(i, carry):
        @pl.when(i != q)
        def _():
            greet(xy_peer(i))

        return carry

    lax.fori_loop(0, NX * NY, greet_xy, 0)

    def greet_z(i, carry):
        @pl.when(i != z)
        def _():
            greet(z_peer(i))

        return carry

    lax.fori_loop(0, NZ, greet_z, 0)

    waves = wave_ref[...].astype(F32)
    kx = waves[0:1] * (4.0 / 1024.0)
    ky = waves[1:2] * (2.0 / 1024.0)
    kz = waves[2:3] * (1.0 / 1024.0)
    shift = jnp.where(c == 0, 0.25, 0.0)
    kv[...] = rows16([kx, ky, kz, kx, ky, kz], K)
    for load in loads:
        load.wait()

    def coords(pos_tile, tile_z):
        px, py, pz = (pos_tile(i).astype(F32) for i in range(3))
        return rows16(
            [
                px,
                py,
                pz,
                (gx * GRID).astype(F32),
                (gy * GRID).astype(F32),
                (tile_z * GRID).astype(F32),
            ],
            TILE,
        )

    own = [coords(lambda i, t=t: halo_pos[4, 1 + t, i], gz * 2 + t) for t in range(2)]

    def tables_k(tile_coords, first):
        def block(b, carry):
            rows = pl.ds(pl.multiple_of(b * 128, 128), 128)
            for t in range(2):
                cycles = lax.dot_general(
                    kv[:, rows], tile_coords[t], FIRST, preferred_element_type=F32
                )
                tab_k[rows, (first + t) * 128 : (first + t + 1) * 128] = sine_of_cycles(
                    cycles + shift
                ).astype(BF16)
            return carry

        lax.fori_loop(0, K // 128, block, 0)

    tables_k(own, 0)
    own_feat = halo[4, 1:3].reshape(2 * TILE, D)
    charge[0 : 2 * TILE] = jnp.dot(
        own_feat, cw_ref[...], preferred_element_type=F32
    ).astype(BF16)

    pl.semaphore_wait(barrier, 25)

    def remote(src, dst, send, recv, peer):
        return pltpu.make_async_remote_copy(
            src_ref=src,
            dst_ref=dst,
            send_sem=send,
            recv_sem=recv,
            device_id=peer,
            device_id_type=MESH,
        )

    pair_copies = [
        remote(halo.at[4, pl.ds(1, 2)], pair, pair_sem.at[0], pair_sem.at[1], partner),
        remote(
            halo_pos.at[4, pl.ds(1, 2)], pair_pos, pair_sem.at[2], pair_sem.at[3], partner
        ),
    ]
    cross_copies = [
        remote(
            halo.at[4, 1 + c], halo.at[4, 3 - 3 * c], hz_sem.at[0], hz_sem.at[1], cross
        ),
        remote(
            halo_pos.at[4, 1 + c],
            halo_pos.at[4, 3 - 3 * c],
            hz_sem.at[2],
            hz_sem.at[3],
            cross,
        ),
    ]

    def inner(col):
        return [
            remote(
                ref.at[col, 2 - c],
                ref.at[col, 3 * c],
                hc_sem.at[2 * i, col],
                hc_sem.at[2 * i + 1, col],
                partner,
            )
            for i, ref in enumerate((halo, halo_pos))
        ]

    def to_y(up):
        col, peer = (3, gy_up) if up else (5, gy_down)
        return [
            remote(
                ref.at[4, pl.ds(c, 3)],
                ref.at[col, pl.ds(c, 3)],
                hy_sem.at[2 * i, up],
                hy_sem.at[2 * i + 1, up],
                peer,
            )
            for i, ref in enumerate((halo, halo_pos))
        ]

    def to_x(up, k):
        peer = gx_up if up else gx_down
        return [
            remote(
                ref.at[3 + k, pl.ds(c, 3)],
                ref.at[(0 if up else 6) + k, pl.ds(c, 3)],
                hx_sem.at[2 * i, 3 * up + k],
                hx_sem.at[2 * i + 1, 3 * up + k],
                peer,
            )
            for i, ref in enumerate((halo, halo_pos))
        ]

    def start(copies):
        for copy in copies:
            copy.start()

    def arrived(copies):
        for copy in copies:
            copy.wait_recv()

    def sent(copies):
        for copy in copies:
            copy.wait_send()

    start(pair_copies)
    start(cross_copies)
    start(inner(4))

    arrived(pair_copies)
    other = [
        coords(lambda i, t=t: pair_pos[t, i], (gz + 1 - 2 * c) * 2 + t) for t in range(2)
    ]
    charge[2 * TILE :] = jnp.dot(
        pair[...].reshape(2 * TILE, D), cw_ref[...], preferred_element_type=F32
    ).astype(BF16)
    tables_k(other, 2)

    def rs_copy(i):
        return remote(
            rs_send.at[i], rs_recv.at[q], coll_sem.at[0], coll_sem.at[1], xy_peer(i)
        )

    def factor_block(b, carry):
        rows = pl.ds(pl.multiple_of(b * 128, 128), 128)
        part = jnp.dot(tab_k[rows, :], charge[...], preferred_element_type=F32)
        rs_send[pl.ds(b * 2, 2)] = part.astype(BF16).reshape(2, 64, D)
        for h in range(2):
            @pl.when(b * 2 + h != q)
            def _():
                rs_copy(b * 2 + h).start()

        return carry

    lax.fori_loop(0, K // 128, factor_block, 0)
    rs_recv[q] = rs_send[q]

    def all_but_one(buffer, n, sem):
        whole = buffer.at[pl.ds(0, n - 1)]
        pltpu.make_async_copy(whole, whole, sem).wait()

    arrived(cross_copies)
    start(to_y(1))
    start(to_y(0))
    start(to_x(1, 1))
    start(to_x(0, 1))

    def centre_rows(t):
        px = halo_pos[4, 1 + t, 0] - 32
        py = halo_pos[4, 1 + t, 1] - 32
        pz = halo_pos[4, 1 + t, 2] + (GRID * t - 64)
        norm = px * px + py * py + pz * pz
        high = (norm >> 8) << 8
        scale = 1.0 / 64.0
        values = [-2 * px, -2 * py, -2 * pz, high, norm - high]
        return rows16([v.astype(F32) * scale for v in values] + [scale, scale], TILE)

    targets = [centre_rows(t) for t in range(2)]

    def column(col, first):
        dx, dy = col // 3 - 1, col % 3 - 1
        px = lanes([halo_pos[col, s, 0] for s in range(4)]) + (dx * GRID - 32)
        py = lanes([halo_pos[col, s, 1] for s in range(4)]) + (dy * GRID - 32)
        pz = lanes([halo_pos[col, s, 2] + (GRID * s - 128) for s in range(4)])
        norm = px * px + py * py + pz * pz
        high = (norm >> 8) << 8
        scale = 1.0 / 64.0
        xs, ys, zs, hs, ls = (
            v.astype(F32) * scale for v in (px, py, pz, high, norm - high)
        )
        sources = rows16([xs, ys, zs, scale, scale, hs, ls], 4 * TILE)
        for t, rad in enumerate((rad0, rad1)):
            q2[t] = lax.dot_general(
                targets[t],
                sources[:, t * TILE : (t + 3) * TILE],
                FIRST,
                preferred_element_type=F32,
            )
            for part in range(8):
                rows = slice(part * 16, part * 16 + 16)
                raw = q2[t, rows]
                s2 = jnp.clip(raw, 1.0 / 8192.0, 1.0)
                s = s2 * lax.rsqrt(s2)
                rest = 1.0 - s2
                env = jnp.where(raw > 0.0, rest * rest, 0.0)
                step = jnp.exp2(s * (6.0 * LOG2E))
                value = env * jnp.exp2(s * (3.0 * LOG2E) - s2 * (18.0 * LOG2E))
                for r in range(NRBF):
                    rad[r * TILE + part * 16 : r * TILE + part * 16 + 16] = value.astype(
                        BF16
                    )
                    if r < NRBF - 1:
                        value = value * step
            near = halo[col, t : t + 3].reshape(3 * TILE, D)
            got = jnp.dot(rad[...], near, preferred_element_type=F32)
            if first:
                pool[t] = got
            else:
                pool[t] += got

    arrived(inner(4))
    column(4, True)

    everyone = lanes(own + other)
    for t in range(4):
        def block(b, carry, t=t):
            cols = pl.ds(pl.multiple_of(b * 128, 128), 128)
            cycles = lax.dot_general(
                everyone[:, t * TILE : (t + 1) * TILE],
                kv[:, cols],
                FIRST,
                preferred_element_type=F32,
            )
            tab_i[t * TILE : (t + 1) * TILE, cols] = sine_of_cycles(
                cycles + shift
            ).astype(BF16)
            return carry

        lax.fori_loop(0, K // 128, block, 0)

    for up, k in ((1, 0), (0, 2)):
        arrived(to_y(up))
        start(inner(3 + k))
        start(to_x(1, k))
        start(to_x(0, k))

    all_but_one(rs_recv, NX * NY, coll_sem.at[1])
    acc = rs_recv[0].astype(F32)
    for i in range(1, NX * NY):
        acc = acc + rs_recv[i].astype(F32)
    rz_send[...] = acc.reshape(NZ, 8, D)

    def rz_copy(i):
        return remote(rz_send.at[i], rz_recv.at[z], coll_sem.at[2], coll_sem.at[3], z_peer(i))

    def send_z(copy_of):
        def one(i, carry):
            @pl.when(i != z)
            def _():
                copy_of(i).start()

            return carry

        lax.fori_loop(0, NZ, one, 0)

    send_z(rz_copy)
    rz_recv[z] = rz_send[z]

    for k in (3, 5):
        arrived(inner(k))
        column(k, False)

    all_but_one(rz_recv, NZ, coll_sem.at[3])
    total = rz_recv[0]
    for i in range(1, NZ):
        total = total + rz_recv[i]
    filt_load.wait()
    factor = total * (1.0 / 256.0)
    filtered = jnp.dot(
        filt[...] * factor,
        mix_ref[...],
        precision=lax.Precision.HIGHEST,
        preferred_element_type=F32,
    )
    gz_send[...] = filtered

    def gz_copy(i):
        return remote(gz_send, gz_recv.at[z], coll_sem.at[4], coll_sem.at[5], z_peer(i))

    send_z(gz_copy)
    gz_recv[z] = filtered

    def relay(up):
        for k in (1, 0, 2):
            arrived(to_x(up, k))
            start(inner((0 if up else 6) + k))

    def side(up):
        for k in (1, 0, 2):
            arrived(inner((0 if up else 6) + k))
            column((0 if up else 6) + k, False)

    relay(1)
    relay(0)

    all_but_one(gz_recv, NZ, coll_sem.at[5])
    block = gz_recv[...].reshape(64, D).astype(BF16)
    ga_send[...] = block

    def ga_copy(i):
        return remote(ga_send, ga_recv.at[q], coll_sem.at[6], coll_sem.at[7], xy_peer(i))

    def send_xy(i, carry):
        @pl.when(i != q)
        def _():
            ga_copy(i).start()

        return carry

    lax.fori_loop(0, NX * NY, send_xy, 0)
    ga_recv[q] = block
    side(1)
    side(0)

    for t in range(2):
        message = jnp.zeros((TILE, D), F32)
        for r in range(NRBF):
            weight = math.exp(-18.0 * ((r + 0.5) / NRBF) ** 2)
            pooled = (pool[t, r * TILE : (r + 1) * TILE] * weight).astype(BF16)
            message = message + jnp.dot(
                pooled, rmix_ref[r * D : (r + 1) * D], preferred_element_type=F32
            )
        far[t * TILE : (t + 1) * TILE] = message + halo[4, 1 + t].astype(F32)

    all_but_one(ga_recv, NX * NY, coll_sem.at[7])
    spectrum = ga_recv[...].reshape(K, D)
    ls_send[...] = jnp.dot(
        tab_i[2 * TILE :], spectrum, preferred_element_type=F32
    )
    last = remote(ls_send, ls_recv, coll_sem.at[8], coll_sem.at[9], partner)
    last.start()
    summed = far[...] + jnp.dot(tab_i[: 2 * TILE], spectrum, preferred_element_type=F32)
    last.wait_recv()
    summed = summed + ls_recv[...]
    mean = jnp.mean(summed * summed, axis=-1, keepdims=True)
    normed = summed * lax.rsqrt(mean + EPS) * gain_ref[...]
    hidden = jnp.dot(normed.astype(BF16), up_ref[...], preferred_element_type=F32)
    hidden = hidden / (1.0 + jnp.exp(-hidden))
    updated = summed + jnp.dot(
        hidden.astype(BF16), down_ref[...], preferred_element_type=F32
    )
    out_ref[...] = updated.astype(BF16).reshape(2, TILE, D)

    sent(pair_copies)
    sent(cross_copies)
    for up in (0, 1):
        sent(to_y(up))
        for k in range(3):
            sent(to_x(up, k))
    for col in range(9):
        sent(inner(col))
    all_but_one(rs_send, NX * NY, coll_sem.at[0])
    all_but_one(rz_send, NZ, coll_sem.at[2])
    all_but_one(gz_recv, NZ, coll_sem.at[4])
    all_but_one(ga_recv, NX * NY, coll_sem.at[6])
    last.wait_send()


def on_device(features, positions, waves, rmix, cw, filters, mix, gain, up, down):
    feat = features.reshape(2, TILE, D)
    pos = positions.reshape(3, 2, 1, TILE).transpose(1, 0, 2, 3)
    vmem = pl.BlockSpec(memory_space=pltpu.VMEM)
    hbm = pl.BlockSpec(memory_space=pl.ANY)
    dma = pltpu.SemaphoreType.DMA
    out = pl.pallas_call(
        kernel,
        out_shape=jax.ShapeDtypeStruct((2, TILE, D), BF16),
        in_specs=[hbm, hbm, vmem, vmem, vmem, hbm, vmem, vmem, vmem, vmem],
        out_specs=vmem,
        scratch_shapes=[
            pltpu.VMEM((9, 4, TILE, D), BF16),
            pltpu.VMEM((9, 4, 3, 1, TILE), jnp.int32),
            pltpu.VMEM((2, TILE, D), BF16),
            pltpu.VMEM((2, 3, 1, TILE), jnp.int32),
            pltpu.VMEM((K, 4 * TILE), BF16),
            pltpu.VMEM((4 * TILE, K), BF16),
            pltpu.VMEM((16, 64, D), BF16),
            pltpu.VMEM((16, 64, D), BF16),
            pltpu.VMEM((NZ, 8, D), F32),
            pltpu.VMEM((NZ, 8, D), F32),
            pltpu.VMEM((8, D), F32),
            pltpu.VMEM((8, D), F32),
            pltpu.VMEM((NZ, 8, D), F32),
            pltpu.VMEM((64, D), BF16),
            pltpu.VMEM((16, 64, D), BF16),
            pltpu.VMEM((2 * TILE, D), F32),
            pltpu.VMEM((2 * TILE, D), F32),
            pltpu.VMEM((16, K), BF16),
            pltpu.VMEM((4 * TILE, D), BF16),
            pltpu.VMEM((2, TILE, 3 * TILE), F32),
            pltpu.VMEM((NRBF * TILE, 3 * TILE), BF16),
            pltpu.VMEM((NRBF * TILE, 3 * TILE), BF16),
            pltpu.VMEM((2, NRBF * TILE, D), F32),
            pltpu.VMEM((2 * TILE, D), F32),
            dma((2,)),
            dma,
            dma((4,)),
            dma((4,)),
            dma((4, 2)),
            dma((4, 6)),
            dma((4, 9)),
            dma((10,)),
        ],
        compiler_params=pltpu.CompilerParams(collective_id=0, has_side_effects=True),
    )(feat, pos, waves, rmix, cw, filters, mix, gain.reshape(1, D), up, down)
    return out.reshape(features.shape)


def solution(mesh):
    tiles = P("gx", "gy", "gz", None, None)
    in_specs = (tiles, P(None, "gx", "gy", "gz", None)) + (P(),) * 8
    return jax.shard_map(
        on_device, mesh=mesh, in_specs=in_specs, out_specs=tiles, check_vma=False
    )
```

```python
import functools
import math

import jax
import jax.numpy as jnp
from jax import lax
from jax.experimental import pallas as pl
from jax.experimental.pallas import tpu as pltpu
from jax.sharding import PartitionSpec as P

MESH = pl.DeviceIdType.MESH
F32, BF16 = jnp.float32, jnp.bfloat16
NRBF = 6
GRID = 64
TILE = 128
D = 128
K = 1024
EPS = 1e-06
NX, NY, NZ = 4, 4, 8
LOG2E = 1.4426950408889634
ROUND = 12582912.0
SIN = (
    6.283182818518357,
    -41.341421396050286,
    81.5961838134782,
    -76.58009997779837,
    41.20539265997673,
    -12.271259128462068,
)
FIRST = (((0,), (0,)), ((), ()))


def rows16(values, width):
    row = lax.broadcasted_iota(jnp.int32, (16, width), 0)
    out = jnp.zeros((16, width), F32)
    for at, value in enumerate(values):
        out = jnp.where(row == at, value, out)
    return out


def sine_of_cycles(cycles):
    f = cycles - ((cycles + ROUND) - ROUND)
    u = f * f
    acc = SIN[5]
    for c in SIN[4::-1]:
        acc = acc * u + c
    return acc * f


def lanes(tiles):
    return jnp.concatenate(tiles, axis=1)


def kernel(
    feat_hbm,
    pos_hbm,
    wave_hbm,
    cw_hbm,
    filt_hbm,
    mix_hbm,
    rmix_hbm,
    gain_hbm,
    up_hbm,
    down_hbm,
    out_ref,
    pos_own,
    wave_ref,
    cw_ref,
    filt,
    mix_ref,
    rmix_ref,
    gain_ref,
    up_ref,
    down_ref,
    halo,
    halo_pos,
    pair_pos,
    tab_i,
    sx_send,
    sx_recv,
    s_own,
    rs_send,
    rs_recv,
    rz_send,
    rz_recv,
    ga_send,
    ga_recv,
    ls_send,
    ls_recv,
    kv,
    kt,
    ct,
    charge,
    q2,
    rad0,
    rad1,
    pool,
    far,
    load_sem,
    pair_sem,
    hz_sem,
    hy_sem,
    hx_sem,
    hc_sem,
    sx_sem,
    coll_sem,
):
    gx, gy, gz = lax.axis_index("gx"), lax.axis_index("gy"), lax.axis_index("gz")
    y, zl, zh, c = gy // 2, gy % 2, gz // 2, gz % 2
    z = zh * 2 + zl
    q = gx * NY + y

    def at(gx_, gy_, gz_):
        return {"gx": gx_, "gy": gy_, "gz": gz_}

    def xy_peer(i):
        return at(i // NY, (i % NY) * 2 + zl, gz)

    def z_peer(i):
        return at(gx, y * 2 + i % 2, (i // 2) * 2 + c)

    partner = at(gx, gy, gz + 1 - 2 * c)
    cross = at(gx, gy, (gz + 2 * c + 7) % 8)
    gy_up, gy_down = at(gx, (gy + 1) % 8, gz), at(gx, (gy + 7) % 8, gz)
    gx_up, gx_down = at((gx + 1) % 4, gy, gz), at((gx + 3) % 4, gy, gz)
    far_y = at(gx, (gy + 2 * zl + 7) % 8, gz)

    barrier = pltpu.get_barrier_semaphore()

    def greet(peer):
        pl.semaphore_signal(barrier, inc=1, device_id=peer, device_id_type=MESH)

    mine = pl.multiple_of(q * 64, 64)
    pairs = [
        (pos_hbm, pos_own),
        (wave_hbm, wave_ref),
        (feat_hbm, halo.at[4, pl.ds(1, 2)]),
        (cw_hbm, cw_ref),
        (filt_hbm.at[pl.ds(mine, 64)], filt),
        (mix_hbm, mix_ref),
        (rmix_hbm, rmix_ref),
        (gain_hbm, gain_ref),
        (up_hbm, up_ref),
        (down_hbm, down_ref),
    ]
    loads = [
        pltpu.make_async_copy(src, dst, load_sem.at[i])
        for i, (src, dst) in enumerate(pairs)
    ]
    for load in loads[:4]:
        load.start()

    greet(partner)
    greet(cross)
    greet(far_y)

    for i in range(1, NX * NY):
        greet(at((gx + i // NY) % NX, (y + i % NY) % NY * 2 + zl, gz))
    for i in range(1, NZ):
        greet(z_peer((z + i) % NZ))
    for load in loads[4:]:
        load.start()

    for load in loads[:2]:
        load.wait()
    waves = wave_ref[...].astype(F32)
    kx = waves[0:1] * (4.0 / 1024.0)
    ky = waves[1:2] * (2.0 / 1024.0)
    kz = waves[2:3] * (1.0 / 1024.0)
    waves = rows16([kx, ky, kz, kx, ky, kz, 1.0], K)
    kv[...] = waves.astype(BF16)
    kt[...] = waves.T.astype(BF16)
    quarter = jnp.where(c == 0, 0.25, 0.0)

    def coords(px, py, pz, tile_z, shift):
        offsets = [(v * GRID).astype(F32) for v in (gx, gy, tile_z)]
        return rows16(
            [px.astype(F32), py.astype(F32), pz.astype(F32)] + offsets + [shift], TILE
        )

    for t in range(2):
        for i in range(3):
            halo_pos[4, 1 + t, i] = pos_own[i, t : t + 1]

    def own_coords(shift):
        return [
            coords(*(halo_pos[4, 1 + t, i] for i in range(3)), gz * 2 + t, shift)
            for t in range(2)
        ]

    own = own_coords(quarter)
    own_half = lanes(own).astype(BF16)
    other_half = lanes(own_coords(0.25 - quarter)).astype(BF16)
    for load in loads[2:4]:
        load.wait()
    own_feat = halo[4, 1:3].reshape(2 * TILE, D)
    charge[...] = jnp.dot(own_feat, cw_ref[...], preferred_element_type=F32).astype(BF16)

    def factors(b, atoms):
        rows = pl.ds(pl.multiple_of(b * 128, 128), 128)
        cycles = jnp.dot(kt[rows], atoms, preferred_element_type=F32)
        table = sine_of_cycles(cycles).astype(BF16)
        return rows, jnp.dot(table, charge[...], preferred_element_type=F32)

    def other_block(b, carry):
        rows, part = factors(b, other_half)
        sx_send[rows] = part.astype(BF16)
        return carry

    lax.fori_loop(0, K // 128, other_block, 0, unroll=True)

    pl.semaphore_wait(barrier, 25)

    def remote(src, dst, send, recv, peer):
        return pltpu.make_async_remote_copy(
            src_ref=src,
            dst_ref=dst,
            send_sem=send,
            recv_sem=recv,
            device_id=peer,
            device_id_type=MESH,
        )

    swap = [
        remote(
            sx_send.at[pl.ds(i * 256, 256)],
            sx_recv.at[pl.ds(i * 256, 256)],
            sx_sem.at[0, i],
            sx_sem.at[1, i],
            partner,
        )
        for i in range(4)
    ]
    pair_copies = [
        remote(
            halo_pos.at[4, pl.ds(1, 2)], pair_pos, pair_sem.at[0], pair_sem.at[1], partner
        )
    ]
    cross_copies = [
        remote(
            halo.at[4, 1 + c], halo.at[4, 3 - 3 * c], hz_sem.at[0], hz_sem.at[1], cross
        ),
        remote(
            halo_pos.at[4, 1 + c],
            halo_pos.at[4, 3 - 3 * c],
            hz_sem.at[2],
            hz_sem.at[3],
            cross,
        ),
    ]

    def inner(col):
        return [
            remote(
                ref.at[col, 2 - c],
                ref.at[col, 3 * c],
                hc_sem.at[2 * i, col],
                hc_sem.at[2 * i + 1, col],
                partner,
            )
            for i, ref in enumerate((halo, halo_pos))
        ]

    def slots(ref, col, end):
        return ref.at[col, 3 * c] if end else ref.at[col, pl.ds(1, 2)]

    def to_y(up, end):
        col, peer = (3, gy_up) if up else (5, gy_down)
        return [
            remote(
                slots(ref, 4, end),
                slots(ref, col, end),
                hy_sem.at[4 * end + 2 * i, up],
                hy_sem.at[4 * end + 2 * i + 1, up],
                peer,
            )
            for i, ref in enumerate((halo, halo_pos))
        ]

    def to_x(up, k, end):
        peer = gx_up if up else gx_down
        return [
            remote(
                slots(ref, 3 + k, end),
                slots(ref, (0 if up else 6) + k, end),
                hx_sem.at[4 * end + 2 * i, 3 * up + k],
                hx_sem.at[4 * end + 2 * i + 1, 3 * up + k],
                peer,
            )
            for i, ref in enumerate((halo, halo_pos))
        ]

    def start(copies):
        for copy in copies:
            copy.start()

    def arrived(copies):
        for copy in copies:
            copy.wait_recv()

    def sent(copies):
        for copy in copies:
            copy.wait_send()

    start(cross_copies)
    start(pair_copies)
    for up in (1, 0):
        start(to_y(up, 0))
        start(to_x(up, 1, 0))
    start(swap)
    start(inner(4))

    def own_block(b, carry):
        rows, part = factors(b, own_half)
        s_own[rows] = part
        return carry

    lax.fori_loop(0, K // 128, own_block, 0, unroll=True)

    def rs_copy(i):
        return remote(
            rs_send.at[i], rs_recv.at[q], coll_sem.at[0], coll_sem.at[1], xy_peer(i)
        )

    for i in range(4):
        arrived(swap[i : i + 1])
        rows = slice(i * 256, i * 256 + 256)
        both = s_own[rows] + sx_recv[rows].astype(F32)
        rs_send[i * 4 : i * 4 + 4] = both.astype(BF16).reshape(4, 64, D)
        for h in range(4):
            @pl.when(i * 4 + h != q)
            def _():
                rs_copy(i * 4 + h).start()

    rs_recv[q] = rs_send[q]

    def all_but_one(buffer, n, sem):
        whole = buffer.at[pl.ds(0, n - 1)]
        pltpu.make_async_copy(whole, whole, sem).wait()

    def centre_rows(t):
        px = halo_pos[4, 1 + t, 0] - 32
        py = halo_pos[4, 1 + t, 1] - 32
        pz = halo_pos[4, 1 + t, 2] + (GRID * t - 64)
        norm = px * px + py * py + pz * pz
        high = (norm >> 8) << 8
        scale = 1.0 / 64.0
        values = [-2 * px, -2 * py, -2 * pz, high, norm - high]
        values = [v.astype(F32) * scale for v in values]
        return rows16(values + [scale, scale], TILE).astype(BF16)

    targets = [centre_rows(t) for t in range(2)]

    def column(col, first):
        dx, dy = col // 3 - 1, col % 3 - 1
        px = lanes([halo_pos[col, s, 0] for s in range(4)]) + (dx * GRID - 32)
        py = lanes([halo_pos[col, s, 1] for s in range(4)]) + (dy * GRID - 32)
        pz = lanes([halo_pos[col, s, 2] + (GRID * s - 128) for s in range(4)])
        norm = px * px + py * py + pz * pz
        high = (norm >> 8) << 8
        scale = 1.0 / 64.0
        xs, ys, zs, hs, ls = (
            v.astype(F32) * scale for v in (px, py, pz, high, norm - high)
        )
        sources = rows16([xs, ys, zs, scale, scale, hs, ls], 4 * TILE).astype(BF16)
        for t, rad in enumerate((rad0, rad1)):
            q2[t] = lax.dot_general(
                targets[t],
                sources[:, t * TILE : (t + 3) * TILE],
                FIRST,
                preferred_element_type=F32,
            )
            for part in range(8):
                rows = slice(part * 16, part * 16 + 16)
                raw = q2[t, rows]
                s2 = jnp.clip(raw, 1.0 / 8192.0, 1.0)
                s = s2 * lax.rsqrt(s2)
                rest = 1.0 - s2
                env = jnp.where(raw > 0.0, rest * rest, 0.0)
                step = jnp.exp2(s * (6.0 * LOG2E))
                value = env * jnp.exp2(s * (3.0 * LOG2E) - s2 * (18.0 * LOG2E))
                for r in range(NRBF):
                    rad[r * TILE + part * 16 : r * TILE + part * 16 + 16] = value.astype(
                        BF16
                    )
                    if r < NRBF - 1:
                        value = value * step
            near = halo[col, t : t + 3].reshape(3 * TILE, D)
            got = jnp.dot(rad[...], near, preferred_element_type=F32)
            if first:
                pool[t] = got
            else:
                pool[t] += got

    arrived(pair_copies)
    other = [
        coords(*(pair_pos[t, i] for i in range(3)), (gz + 1 - 2 * c) * 2 + t, quarter)
        for t in range(2)
    ]
    for t, tile in enumerate(own + other):
        ct[t * TILE : (t + 1) * TILE] = tile.T.astype(BF16)

    def table_block(b, carry):
        rows = pl.ds(pl.multiple_of(b * 64, 64), 64)
        for part in range(4):
            cols = slice(part * 256, part * 256 + 256)
            cycles = jnp.dot(ct[rows], kv[:, cols], preferred_element_type=F32)
            tab_i[rows, cols] = sine_of_cycles(cycles).astype(BF16)
        return carry

    lax.fori_loop(0, 8, table_block, 0)

    arrived(cross_copies)
    for up in (1, 0):
        start(to_y(up, 1))
        start(to_x(up, 1, 1))
    for up, k in ((1, 0), (0, 2)):
        arrived(to_y(up, 0))
        start(inner(3 + k))
        start(to_x(1, k, 0))
        start(to_x(0, k, 0))

    arrived(inner(4))
    column(4, True)

    all_but_one(rs_recv, NX * NY, coll_sem.at[1])
    acc = rs_recv[0].astype(F32)
    for i in range(1, NX * NY):
        acc = acc + rs_recv[i].astype(F32)
    rz_send[...] = acc.astype(BF16)
    rz_recv[z] = rz_send[...]

    def rz_copy(i):
        return remote(rz_send, rz_recv.at[z], coll_sem.at[2], coll_sem.at[3], z_peer(i))

    def send_z(i, carry):
        @pl.when(i != z)
        def _():
            rz_copy(i).start()

        return carry

    lax.fori_loop(0, NZ, send_z, 0)

    for up, k in ((1, 0), (0, 2)):
        arrived(to_y(up, 1))
        start(to_x(1, k, 1))
        start(to_x(0, k, 1))
    for up, col in ((1, 1), (0, 7)):
        arrived(to_x(up, 1, 0))
        start(inner(col))
    for col in (3, 5):
        arrived(inner(col))
        column(col, False)
    for up, col in ((1, 1), (0, 7)):
        arrived(to_x(up, 1, 1))
        arrived(inner(col))
        column(col, False)
    for load in loads[4:]:
        load.wait()
    mix_high = mix_ref[...].astype(BF16)
    mix_low = (mix_ref[...] - mix_high.astype(F32)).astype(BF16)

    all_but_one(rz_recv, NZ, coll_sem.at[3])
    total = rz_recv[0].astype(F32)
    for i in range(1, NZ):
        total = total + rz_recv[i].astype(F32)
    product = filt[...] * (total * (1.0 / 256.0))
    high = product.astype(BF16)
    low = (product - high.astype(F32)).astype(BF16)
    block = (
        jnp.dot(high, mix_high, preferred_element_type=F32)
        + jnp.dot(low, mix_high, preferred_element_type=F32)
        + jnp.dot(high, mix_low, preferred_element_type=F32)
    ).astype(BF16)
    ga_send[...] = block

    def ga_copy(i):
        return remote(ga_send, ga_recv.at[q], coll_sem.at[6], coll_sem.at[7], xy_peer(i))

    def send_xy(i, carry):
        @pl.when(i != q)
        def _():
            ga_copy(i).start()

        return carry

    lax.fori_loop(0, NX * NY, send_xy, 0)
    ga_recv[q] = block
    corners = ((1, 0, 0), (1, 2, 2), (0, 0, 6), (0, 2, 8))
    for up, k, col in corners:
        arrived(to_x(up, k, 0))
        start(inner(col))
    for up, k, col in corners:
        arrived(to_x(up, k, 1))
        arrived(inner(col))
        column(col, False)

    for t in range(2):
        message = jnp.zeros((TILE, D), F32)
        for r in range(NRBF):
            weight = math.exp(-18.0 * ((r + 0.5) / NRBF) ** 2)
            pooled = (pool[t, r * TILE : (r + 1) * TILE] * weight).astype(BF16)
            message = message + jnp.dot(
                pooled, rmix_ref[r * D : (r + 1) * D], preferred_element_type=F32
            )
        far[t * TILE : (t + 1) * TILE] = message + halo[4, 1 + t].astype(F32)

    all_but_one(ga_recv, NX * NY, coll_sem.at[7])
    spectrum = ga_recv[...].reshape(K, D)
    ls_send[...] = jnp.dot(
        tab_i[2 * TILE :], spectrum, preferred_element_type=F32
    )
    last = remote(ls_send, ls_recv, coll_sem.at[8], coll_sem.at[9], partner)
    last.start()
    summed = far[...] + jnp.dot(tab_i[: 2 * TILE], spectrum, preferred_element_type=F32)
    last.wait_recv()
    summed = summed + ls_recv[...]
    mean = jnp.mean(summed * summed, axis=-1, keepdims=True)
    normed = summed * lax.rsqrt(mean + EPS) * gain_ref[...]
    hidden = jnp.dot(normed.astype(BF16), up_ref[...], preferred_element_type=F32)
    hidden = hidden / (1.0 + jnp.exp(-hidden))
    updated = summed + jnp.dot(
        hidden.astype(BF16), down_ref[...], preferred_element_type=F32
    )
    out_ref[...] = updated.astype(BF16).reshape(2, TILE, D)

    sent(swap)
    sent(pair_copies)
    sent(cross_copies)
    for up in (0, 1):
        for end in (0, 1):
            sent(to_y(up, end))
            for k in range(3):
                sent(to_x(up, k, end))
    for col in range(9):
        sent(inner(col))
    all_but_one(rs_send, NX * NY, coll_sem.at[0])
    all_but_one(rz_recv, NZ, coll_sem.at[2])
    all_but_one(ga_recv, NX * NY, coll_sem.at[6])
    last.wait_send()


def on_device(features, positions, waves, rmix, cw, filters, mix, gain, up, down):
    feat = features.reshape(2, TILE, D)
    pos = positions.reshape(3, 2, TILE)
    hbm = pl.BlockSpec(memory_space=pl.ANY)
    dma = pltpu.SemaphoreType.DMA
    vmem = pltpu.VMEM
    out = pl.pallas_call(
        kernel,
        out_shape=pltpu.VMEM((2, TILE, D), BF16),
        in_specs=[hbm] * 10,
        out_specs=pl.BlockSpec(memory_space=pltpu.VMEM),
        scratch_shapes=[
            vmem((3, 2, TILE), jnp.int32),
            vmem((3, K), jnp.int32),
            vmem((D, D), BF16),
            vmem((64, D), F32),
            vmem((D, D), F32),
            vmem((NRBF * D, D), BF16),
            vmem((1, D), F32),
            vmem((D, 2 * D), BF16),
            vmem((2 * D, D), BF16),
            vmem((9, 4, TILE, D), BF16),
            vmem((9, 4, 3, 1, TILE), jnp.int32),
            vmem((2, 3, 1, TILE), jnp.int32),
            vmem((4 * TILE, K), BF16),
            vmem((K, D), BF16),
            vmem((K, D), BF16),
            vmem((K, D), F32),
            vmem((16, 64, D), BF16),
            vmem((16, 64, D), BF16),
            vmem((64, D), BF16),
            vmem((NZ, 64, D), BF16),
            vmem((64, D), BF16),
            vmem((16, 64, D), BF16),
            vmem((2 * TILE, D), F32),
            vmem((2 * TILE, D), F32),
            vmem((16, K), BF16),
            vmem((K, 16), BF16),
            vmem((4 * TILE, 16), BF16),
            vmem((2 * TILE, D), BF16),
            vmem((2, TILE, 3 * TILE), F32),
            vmem((NRBF * TILE, 3 * TILE), BF16),
            vmem((NRBF * TILE, 3 * TILE), BF16),
            vmem((2, NRBF * TILE, D), F32),
            vmem((2 * TILE, D), F32),
            dma((10,)),
            dma((2,)),
            dma((4,)),
            dma((8, 2)),
            dma((8, 6)),
            dma((4, 9)),
            dma((2, 4)),
            dma((10,)),
        ],
        compiler_params=pltpu.CompilerParams(collective_id=0, has_side_effects=True),
    )(feat, pos, waves, cw, filters, mix, rmix, gain.reshape(1, D), up, down)
    return out.reshape(features.shape)


def solution(mesh):
    tiles = P("gx", "gy", "gz", None, None)
    in_specs = (tiles, P(None, "gx", "gy", "gz", None)) + (P(),) * 8
    return jax.shard_map(
        on_device, mesh=mesh, in_specs=in_specs, out_specs=tiles, check_vma=False
    )
```

```python
import functools
import math

import jax
import jax.numpy as jnp
from jax import lax
from jax.experimental import pallas as pl
from jax.experimental.pallas import tpu as pltpu
from jax.sharding import PartitionSpec as P

MESH = pl.DeviceIdType.MESH
F32, BF16 = jnp.float32, jnp.bfloat16
NRBF = 6
GRID = 64
TILE = 128
D = 128
K = 1024
EPS = 1e-06
NX, NY, NZ = 4, 4, 8
LOG2E = 1.4426950408889634
ROUND = 12582912.0
SIN = (
    6.283182818518357,
    -41.341421396050286,
    81.5961838134782,
    -76.58009997779837,
    41.20539265997673,
    -12.271259128462068,
)
ORDER = (2, 1, 3, 0)
PLANE = [(i, j) for i in ORDER for j in ORDER if i or j]
LINE = sorted(range(1, 8), key=lambda i: -min(i, 8 - i))
FIRST = (((0,), (0,)), ((), ()))


def rows16(values, width):
    row = lax.broadcasted_iota(jnp.int32, (16, width), 0)
    out = jnp.zeros((16, width), F32)
    for at, value in enumerate(values):
        out = jnp.where(row == at, value, out)
    return out


def sine_of_cycles(cycles):
    f = cycles - ((cycles + ROUND) - ROUND)
    u = f * f
    acc = SIN[5]
    for c in SIN[4::-1]:
        acc = acc * u + c
    return acc * f


def lanes(tiles):
    return jnp.concatenate(tiles, axis=1)


def kernel(
    feat_hbm,
    pos_hbm,
    wave_hbm,
    cw_hbm,
    filt_hbm,
    mix_hbm,
    rmix_hbm,
    gain_hbm,
    up_hbm,
    down_hbm,
    out_ref,
    pos_own,
    wave_ref,
    cw_ref,
    filt,
    mix_ref,
    rmix_ref,
    gain_ref,
    up_ref,
    down_ref,
    halo,
    halo_pos,
    pair_pos,
    tab_i,
    sx_send,
    sx_recv,
    s_own,
    rs_send,
    rs_recv,
    rz_send,
    rz_recv,
    ga_send,
    ga_recv,
    ls_send,
    ls_recv,
    kv,
    kt,
    ct,
    charge,
    q2,
    rad0,
    rad1,
    pool,
    far,
    bytes_of,
    load_sem,
    send_sem,
    pair_sem,
    hz_sem,
    hy_sem,
    hx_sem,
    hc_sem,
    sx_sem,
    coll_sem,
    ga_sem,
    met_sem,
):
    gx, gy, gz = lax.axis_index("gx"), lax.axis_index("gy"), lax.axis_index("gz")
    y, zl, zh, c = gy // 2, gy % 2, gz // 2, gz % 2
    z = zh * 2 + zl
    q = gx * NY + y

    def at(gx_, gy_, gz_):
        return {"gx": gx_, "gy": gy_, "gz": gz_}

    def plane_peer(i, j):
        x_, y_ = (gx + i) % NX, (y + j) % NY
        return x_ * NY + y_, at(x_, y_ * 2 + zl, gz)

    def z_peer(i):
        return at(gx, y * 2 + i % 2, (i // 2) * 2 + c)

    partner = at(gx, gy, gz + 1 - 2 * c)
    cross = at(gx, gy, (gz + 2 * c + 7) % 8)
    gy_up, gy_down = at(gx, (gy + 1) % 8, gz), at(gx, (gy + 7) % 8, gz)
    gx_up, gx_down = at((gx + 1) % 4, gy, gz), at((gx + 3) % 4, gy, gz)
    far_y = at(gx, (gy + 2 * zl + 7) % 8, gz)

    barrier = pltpu.get_barrier_semaphore()

    def signal(sem, peer):
        pl.semaphore_signal(sem, inc=1, device_id=peer, device_id_type=MESH)

    def remote(src, dst, send, recv, peer):
        return pltpu.make_async_remote_copy(
            src_ref=src,
            dst_ref=dst,
            send_sem=send,
            recv_sem=recv,
            device_id=peer,
            device_id_type=MESH,
        )

    def all_of(ref, sem):
        pltpu.make_async_copy(ref, ref, sem).wait()

    mine = pl.multiple_of(q * 64, 64)
    pairs = [
        (pos_hbm, pos_own),
        (wave_hbm, wave_ref),
        (feat_hbm, halo.at[pl.ds(17, 2)]),
        (cw_hbm, cw_ref),
        (filt_hbm.at[pl.ds(mine, 64)], filt),
        (mix_hbm, mix_ref),
        (rmix_hbm, rmix_ref),
        (gain_hbm, gain_ref),
        (up_hbm, up_ref),
        (down_hbm, down_ref),
    ]
    loads = [
        pltpu.make_async_copy(src, dst, load_sem.at[min(i, 4)])
        for i, (src, dst) in enumerate(pairs)
    ]
    for load in loads[:4]:
        load.start()

    for load in loads[4:]:
        load.start()

    @pl.when(c == 1)
    def _():
        signal(barrier, partner)
        pl.semaphore_wait(met_sem, 1)
        for i, j in PLANE:
            signal(barrier, plane_peer(i, j)[1])
        for i in LINE:
            signal(barrier, z_peer((z + i) % NZ))
        signal(barrier, far_y)

    @pl.when(c == 0)
    def _():
        pl.semaphore_wait(barrier, 1)
        signal(met_sem, partner)

    for load in loads[:2]:
        load.wait()
    waves = wave_ref[...].astype(F32)
    kx = waves[0:1] * (4.0 / 1024.0)
    ky = waves[1:2] * (2.0 / 1024.0)
    kz = waves[2:3] * (1.0 / 1024.0)
    waves = rows16([kx, ky, kz, kx, ky, kz, 1.0], K)
    kv[...] = waves
    kt[...] = waves.T.astype(BF16)
    quarter = jnp.where(c == 0, 0.25, 0.0)

    def coords(px, py, pz, tile_z, shift):
        offsets = [(v * GRID).astype(F32) for v in (gx, gy, tile_z)]
        return rows16(
            [px.astype(F32), py.astype(F32), pz.astype(F32)] + offsets + [shift], TILE
        )

    for t in range(2):
        for i in range(3):
            halo_pos[17 + t, i] = pos_own[i, t : t + 1]

    def own_coords(shift):
        return [
            coords(*(halo_pos[17 + t, i] for i in range(3)), gz * 2 + t, shift)
            for t in range(2)
        ]

    own = own_coords(quarter)
    own_half = lanes(own).astype(BF16)
    other_half = lanes(own_coords(0.25 - quarter)).astype(BF16)
    for load in loads[2:4]:
        load.wait()
    own_feat = halo[17:19].reshape(2 * TILE, D)
    charge[...] = jnp.dot(own_feat, cw_ref[...], preferred_element_type=F32).astype(BF16)

    def factors(b, atoms):
        rows = pl.ds(pl.multiple_of(b * 128, 128), 128)
        cycles = jnp.dot(kt[rows], atoms, preferred_element_type=F32)
        table = sine_of_cycles(cycles).astype(BF16)
        return rows, jnp.dot(table, charge[...], preferred_element_type=F32)

    def group(i):
        return pl.multiple_of((gx + i) % NX * 256, 256)

    for i in ORDER:
        for h in range(2):
            rows, part = factors(group(i) // 128 + h, other_half)
            sx_send[rows] = part.astype(BF16)
        rows = pl.ds(group(i), 256)
        remote(
            sx_send.at[rows], sx_recv.at[rows], send_sem.at[2], sx_sem.at[i], partner
        ).start()

    for i in ORDER:
        for h in range(2):
            rows, part = factors(group(i) // 128 + h, own_half)
            s_own[rows] = part

    for i in ORDER:
        rows = pl.ds(group(i), 256)
        all_of(sx_recv.at[rows], sx_sem.at[i])
        both = s_own[rows] + sx_recv[rows].astype(F32)
        rs_send[pl.ds(group(i) // 64, 4)] = both.astype(BF16).reshape(4, 64, D)

    @pl.when(c == 1)
    def _():
        pl.semaphore_wait(barrier, 23)
        signal(met_sem, partner)

    @pl.when(c == 0)
    def _():
        pl.semaphore_wait(met_sem, 1)

    for i, j in PLANE:
        block, peer = plane_peer(i, j)
        remote(
            rs_send.at[block], rs_recv.at[q], coll_sem.at[0], coll_sem.at[1], peer
        ).start()

    def tiles(src, dst, n, sem, peer):
        return [
            remote(
                ref.at[pl.ds(src, n)], ref.at[pl.ds(dst, n)], send_sem.at[i], sem, peer
            )
            for i, ref in enumerate((halo, halo_pos))
        ]

    def got_tiles(n, sem):
        all_of(bytes_of.at[pl.ds(0, 67 * n)], sem)

    pair_copy = remote(
        halo_pos.at[pl.ds(17, 2)], pair_pos, send_sem.at[1], pair_sem, partner
    )

    def inner(col):
        return tiles(col * 4 + 2 - c, col * 4 + 3 * c, 1, hc_sem.at[col], partner)

    def sides(src, dst, end, sem, peer):
        if end:
            return tiles(src * 4 + 3 * c, dst * 4 + 3 * c, 1, sem, peer)
        return tiles(src * 4 + 1, dst * 4 + 1, 2, sem, peer)

    def to_y(up, end):
        col, peer = (3, gy_up) if up else (5, gy_down)
        return sides(4, col, end, hy_sem.at[end, up], peer)

    def to_x(up, k, end):
        peer = gx_up if up else gx_down
        dst = (0 if up else 6) + k
        return sides(3 + k, dst, end, hx_sem.at[end, 3 * up + k], peer)

    def start(copies):
        for copy in copies:
            copy.start()

    def got_y(up, end):
        got_tiles(2 - end, hy_sem.at[end, up])

    def got_x(up, k, end):
        got_tiles(2 - end, hx_sem.at[end, 3 * up + k])

    def got_inner(col):
        got_tiles(1, hc_sem.at[col])

    start(tiles(17 + c, 19 - 3 * c, 1, hz_sem, cross))
    pair_copy.start()
    for up in (1, 0):
        start(to_y(up, 0))
        start(to_x(up, 1, 0))
    start(inner(4))
    rs_recv[q] = rs_send[q]

    def all_but_one(buffer, n, sem):
        all_of(buffer.at[pl.ds(0, n - 1)], sem)

    def centre_rows(t):
        px = halo_pos[17 + t, 0] - 32
        py = halo_pos[17 + t, 1] - 32
        pz = halo_pos[17 + t, 2] + (GRID * t - 64)
        norm = px * px + py * py + pz * pz
        high = (norm >> 8) << 8
        scale = 1.0 / 64.0
        values = [-2 * px, -2 * py, -2 * pz, high, norm - high]
        values = [v.astype(F32) * scale for v in values]
        return rows16(values + [scale, scale], TILE).astype(BF16)

    targets = [centre_rows(t) for t in range(2)]

    def column(col, first):
        dx, dy = col // 3 - 1, col % 3 - 1
        px = lanes([halo_pos[col * 4 + s, 0] for s in range(4)]) + (dx * GRID - 32)
        py = lanes([halo_pos[col * 4 + s, 1] for s in range(4)]) + (dy * GRID - 32)
        pz = lanes([halo_pos[col * 4 + s, 2] + (GRID * s - 128) for s in range(4)])
        norm = px * px + py * py + pz * pz
        high = (norm >> 8) << 8
        scale = 1.0 / 64.0
        xs, ys, zs, hs, ls = (
            v.astype(F32) * scale for v in (px, py, pz, high, norm - high)
        )
        sources = rows16([xs, ys, zs, scale, scale, hs, ls], 4 * TILE).astype(BF16)
        for t, rad in enumerate((rad0, rad1)):
            q2[t] = lax.dot_general(
                targets[t],
                sources[:, t * TILE : (t + 3) * TILE],
                FIRST,
                preferred_element_type=F32,
            )
            for part in range(8):
                rows = slice(part * 16, part * 16 + 16)
                raw = q2[t, rows]
                s2 = jnp.clip(raw, 1.0 / 8192.0, 1.0)
                s = s2 * lax.rsqrt(s2)
                rest = 1.0 - s2
                env = jnp.where(raw > 0.0, rest * rest, 0.0)
                step = jnp.exp2(s * (6.0 * LOG2E))
                value = env * jnp.exp2(s * (3.0 * LOG2E) - s2 * (18.0 * LOG2E))
                for r in range(NRBF):
                    rad[r * TILE + part * 16 : r * TILE + part * 16 + 16] = value.astype(
                        BF16
                    )
                    if r < NRBF - 1:
                        value = value * step
            near = halo[col * 4 + t : col * 4 + t + 3].reshape(3 * TILE, D)
            got = jnp.dot(rad[...], near, preferred_element_type=F32)
            if first:
                pool[t] = got
            else:
                pool[t] += got

    pair_copy.wait_recv()
    other = [
        coords(*(pair_pos[t, i] for i in range(3)), (gz + 1 - 2 * c) * 2 + t, quarter)
        for t in range(2)
    ]
    for t, tile in enumerate(own + other):
        ct[t * TILE : (t + 1) * TILE] = tile.T.astype(BF16)

    turned = []
    for i in range(4):
        part = kv[:, pl.ds(group(i), 256)]
        turned.append(pltpu.roll(part, (NY - y) % NY * 64, axis=1).astype(BF16))

    def table_block(b, carry):
        rows = pl.ds(pl.multiple_of(b * 64, 64), 64)
        for part in range(4):
            cols = slice(part * 256, part * 256 + 256)
            cycles = jnp.dot(ct[rows], turned[part], preferred_element_type=F32)
            tab_i[rows, cols] = sine_of_cycles(cycles).astype(BF16)
        return carry

    lax.fori_loop(0, 8, table_block, 0)

    got_tiles(1, hz_sem)
    for up in (1, 0):
        start(to_y(up, 1))
        start(to_x(up, 1, 1))

    got_inner(4)
    column(4, True)

    all_but_one(rs_recv, NX * NY, coll_sem.at[1])
    acc = rs_recv[0].astype(F32)
    for i in range(1, NX * NY):
        acc = acc + rs_recv[i].astype(F32)
    rz_send[...] = acc.astype(BF16)
    rz_recv[z] = rz_send[...]

    for i in LINE:
        remote(
            rz_send,
            rz_recv.at[z],
            coll_sem.at[2],
            coll_sem.at[3],
            z_peer((z + i) % NZ),
        ).start()

    for up, k in ((1, 0), (0, 2)):
        got_y(up, 0)
        start(inner(3 + k))
        start(to_x(1, k, 0))
        start(to_x(0, k, 0))
    for up, col in ((1, 1), (0, 7)):
        got_x(up, 1, 0)
        start(inner(col))
    for up, k in ((1, 0), (0, 2)):
        got_y(up, 1)
        start(to_x(1, k, 1))
        start(to_x(0, k, 1))
    for col in (3, 5):
        got_inner(col)
        column(col, False)
    for up, col in ((1, 1), (0, 7)):
        got_x(up, 1, 1)
        got_inner(col)
        column(col, False)
    all_of(bytes_of, load_sem.at[4])
    mix_high = mix_ref[...].astype(BF16)
    mix_low = (mix_ref[...] - mix_high.astype(F32)).astype(BF16)

    all_but_one(rz_recv, NZ, coll_sem.at[3])
    total = rz_recv[0].astype(F32)
    for i in range(1, NZ):
        total = total + rz_recv[i].astype(F32)
    product = filt[...] * (total * (1.0 / 256.0))
    high = product.astype(BF16)
    low = (product - high.astype(F32)).astype(BF16)
    block = (
        jnp.dot(high, mix_high, preferred_element_type=F32)
        + jnp.dot(low, mix_high, preferred_element_type=F32)
        + jnp.dot(high, mix_low, preferred_element_type=F32)
    ).astype(BF16)
    ga_send[...] = block

    for i, j in PLANE:
        back = (4 - i) % 4
        remote(
            ga_send,
            ga_recv.at[back * 4 + (4 - j) % 4],
            coll_sem.at[4],
            ga_sem.at[back],
            plane_peer(i, j)[1],
        ).start()
    ga_recv[0] = block
    corners = ((1, 0, 0), (1, 2, 2), (0, 0, 6), (0, 2, 8))
    for up, k, col in corners:
        got_x(up, k, 0)
        start(inner(col))
    for up, k, col in corners:
        got_x(up, k, 1)
        got_inner(col)
        column(col, False)

    for t in range(2):
        message = jnp.zeros((TILE, D), F32)
        for r in range(NRBF):
            weight = math.exp(-18.0 * ((r + 0.5) / NRBF) ** 2)
            pooled = (pool[t, r * TILE : (r + 1) * TILE] * weight).astype(BF16)
            message = message + jnp.dot(
                pooled, rmix_ref[r * D : (r + 1) * D], preferred_element_type=F32
            )
        far[t * TILE : (t + 1) * TILE] = message + halo[17 + t].astype(F32)

    theirs, ours = 0.0, far[...]
    for i in (0, 1, 3, 2):
        some = ga_recv.at[pl.ds(i * 4, 4 if i else 3)]
        all_of(some, ga_sem.at[i])
        cols = slice(i * 256, i * 256 + 256)
        spectrum = ga_recv[i * 4 : i * 4 + 4].reshape(256, D)
        theirs = theirs + jnp.dot(
            tab_i[2 * TILE :, cols], spectrum, preferred_element_type=F32
        )
        if i == 2:
            ls_send[...] = theirs
            last = remote(ls_send, ls_recv, coll_sem.at[5], coll_sem.at[6], partner)
            last.start()
        ours = ours + jnp.dot(
            tab_i[: 2 * TILE, cols], spectrum, preferred_element_type=F32
        )
    last.wait_recv()
    summed = ours + ls_recv[...]
    mean = jnp.mean(summed * summed, axis=-1, keepdims=True)
    normed = summed * lax.rsqrt(mean + EPS) * gain_ref[...]
    hidden = jnp.dot(normed.astype(BF16), up_ref[...], preferred_element_type=F32)
    hidden = hidden / (1.0 + jnp.exp(-hidden))
    updated = summed + jnp.dot(
        hidden.astype(BF16), down_ref[...], preferred_element_type=F32
    )
    out_ref[...] = updated.astype(BF16).reshape(2, TILE, D)

    all_of(halo.at[pl.ds(0, 34)], send_sem.at[0])
    all_of(halo_pos, send_sem.at[1])
    all_of(sx_send, send_sem.at[2])
    all_but_one(rs_send, NX * NY, coll_sem.at[0])
    all_but_one(rz_recv, NZ, coll_sem.at[2])
    all_but_one(ga_recv, NX * NY, coll_sem.at[4])
    all_of(ls_send, coll_sem.at[5])


def on_device(features, positions, waves, rmix, cw, filters, mix, gain, up, down):
    feat = features.reshape(2, TILE, D)
    pos = positions.reshape(3, 2, TILE)
    hbm = pl.BlockSpec(memory_space=pl.ANY)
    dma = pltpu.SemaphoreType.DMA
    vmem = pltpu.VMEM
    out = pl.pallas_call(
        kernel,
        out_shape=pltpu.VMEM((2, TILE, D), BF16),
        in_specs=[hbm] * 10,
        out_specs=pl.BlockSpec(memory_space=pltpu.VMEM),
        scratch_shapes=[
            vmem((3, 2, TILE), jnp.int32),
            vmem((3, K), jnp.int32),
            vmem((D, D), BF16),
            vmem((64, D), F32),
            vmem((D, D), F32),
            vmem((NRBF * D, D), BF16),
            vmem((1, D), F32),
            vmem((D, 2 * D), BF16),
            vmem((2 * D, D), BF16),
            vmem((36, TILE, D), BF16),
            vmem((36, 3, 1, TILE), jnp.int32),
            vmem((2, 3, 1, TILE), jnp.int32),
            vmem((4 * TILE, K), BF16),
            vmem((K, D), BF16),
            vmem((K, D), BF16),
            vmem((K, D), F32),
            vmem((16, 64, D), BF16),
            vmem((16, 64, D), BF16),
            vmem((64, D), BF16),
            vmem((NZ, 64, D), BF16),
            vmem((64, D), BF16),
            vmem((16, 64, D), BF16),
            vmem((2 * TILE, D), F32),
            vmem((2 * TILE, D), F32),
            vmem((16, K), F32),
            vmem((K, 16), BF16),
            vmem((4 * TILE, 16), BF16),
            vmem((2 * TILE, D), BF16),
            vmem((2, TILE, 3 * TILE), F32),
            vmem((NRBF * TILE, 3 * TILE), BF16),
            vmem((NRBF * TILE, 3 * TILE), BF16),
            vmem((2, NRBF * TILE, D), F32),
            vmem((2 * TILE, D), F32),
            vmem((833, 1, D), F32),
            dma((5,)),
            dma((3,)),
            dma,
            dma,
            dma((2, 2)),
            dma((2, 6)),
            dma((9,)),
            dma((4,)),
            dma((7,)),
            dma((4,)),
            pltpu.SemaphoreType.REGULAR,
        ],
        compiler_params=pltpu.CompilerParams(collective_id=0, has_side_effects=True),
    )(feat, pos, waves, cw, filters, mix, rmix, gain.reshape(1, D), up, down)
    return out.reshape(features.shape)


def solution(mesh):
    tiles = P("gx", "gy", "gz", None, None)
    in_specs = (tiles, P(None, "gx", "gy", "gz", None)) + (P(),) * 8
    return jax.shard_map(
        on_device, mesh=mesh, in_specs=in_specs, out_specs=tiles, check_vma=False
    )
```

```python
import functools
import math

import jax
import jax.numpy as jnp
from jax import lax
from jax.experimental import pallas as pl
from jax.experimental.pallas import tpu as pltpu
from jax.sharding import PartitionSpec as P

MESH = pl.DeviceIdType.MESH
F32, BF16 = jnp.float32, jnp.bfloat16
NRBF = 6
GRID = 64
TILE = 128
D = 128
K = 1024
EPS = 1e-06
NX, NY, NZ = 4, 4, 8
LOG2E = 1.4426950408889634
ROUND = 12582912.0
SIN = (
    6.283182818518357,
    -41.341421396050286,
    81.5961838134782,
    -76.58009997779837,
    41.20539265997673,
    -12.271259128462068,
)
ORDER = (2, 1, 3, 0)
PLANE = [(i, j) for i in ORDER for j in ORDER if i or j]
LINE = sorted(range(1, 8), key=lambda i: -min(i, 8 - i))
FIRST = (((0,), (0,)), ((), ()))


def rows16(values, width):
    row = lax.broadcasted_iota(jnp.int32, (16, width), 0)
    out = jnp.zeros((16, width), F32)
    for at, value in enumerate(values):
        out = jnp.where(row == at, value, out)
    return out


def sine_of_cycles(cycles):
    f = cycles - ((cycles + ROUND) - ROUND)
    u = f * f
    acc = SIN[5]
    for c in SIN[4::-1]:
        acc = acc * u + c
    return acc * f


def lanes(tiles):
    return jnp.concatenate(tiles, axis=1)


def kernel(
    feat_hbm,
    pos_hbm,
    wave_hbm,
    cw_hbm,
    filt_hbm,
    mix_hbm,
    rmix_hbm,
    gain_hbm,
    up_hbm,
    down_hbm,
    out_ref,
    pos_own,
    wave_ref,
    cw_ref,
    filt,
    mix_ref,
    rmix_ref,
    gain_ref,
    up_ref,
    down_ref,
    halo,
    halo_pos,
    pair_pos,
    tab_i,
    sx_send,
    sx_recv,
    s_own,
    rs_send,
    rs_recv,
    rz_send,
    rz_recv,
    ga_send,
    ga_recv,
    ls_send,
    ls_recv,
    kv,
    kt,
    ct,
    charge,
    q2,
    targets,
    rad0,
    rad1,
    rad2,
    rad3,
    pool,
    far,
    bytes_of,
    load_sem,
    send_sem,
    pair_sem,
    hz_sem,
    hy_sem,
    hx_sem,
    hc_sem,
    sx_sem,
    coll_sem,
    ga_sem,
    met_sem,
):
    gx, gy, gz = lax.axis_index("gx"), lax.axis_index("gy"), lax.axis_index("gz")
    y, zl, zh, c = gy // 2, gy % 2, gz // 2, gz % 2
    z = zh * 2 + zl
    q = gx * NY + y

    def at(gx_, gy_, gz_):
        return {"gx": gx_, "gy": gy_, "gz": gz_}

    def plane_peer(i, j):
        x_, y_ = (gx + i) % NX, (y + j) % NY
        return x_ * NY + y_, at(x_, y_ * 2 + zl, gz)

    def z_peer(i):
        return at(gx, y * 2 + i % 2, (i // 2) * 2 + c)

    partner = at(gx, gy, gz + 1 - 2 * c)
    cross = at(gx, gy, (gz + 2 * c + 7) % 8)
    gy_up, gy_down = at(gx, (gy + 1) % 8, gz), at(gx, (gy + 7) % 8, gz)
    gx_up, gx_down = at((gx + 1) % 4, gy, gz), at((gx + 3) % 4, gy, gz)
    far_y = at(gx, (gy + 2 * zl + 7) % 8, gz)

    barrier = pltpu.get_barrier_semaphore()

    def signal(sem, peer):
        pl.semaphore_signal(sem, inc=1, device_id=peer, device_id_type=MESH)

    def remote(src, dst, send, recv, peer):
        return pltpu.make_async_remote_copy(
            src_ref=src,
            dst_ref=dst,
            send_sem=send,
            recv_sem=recv,
            device_id=peer,
            device_id_type=MESH,
        )

    def all_of(ref, sem):
        pltpu.make_async_copy(ref, ref, sem).wait()

    mine = pl.multiple_of(q * 64, 64)
    pairs = [
        (pos_hbm, pos_own),
        (wave_hbm, wave_ref),
        (feat_hbm, halo.at[pl.ds(17, 2)]),
        (cw_hbm, cw_ref),
        (filt_hbm.at[pl.ds(mine, 64)], filt),
        (mix_hbm, mix_ref),
        (rmix_hbm, rmix_ref),
        (gain_hbm, gain_ref),
        (up_hbm, up_ref),
        (down_hbm, down_ref),
    ]
    loads = [
        pltpu.make_async_copy(src, dst, load_sem.at[min(i, 4)])
        for i, (src, dst) in enumerate(pairs)
    ]
    for load in loads[:4]:
        load.start()

    for load in loads[4:]:
        load.start()

    @pl.when(c == 1)
    def _():
        signal(barrier, partner)
        pl.semaphore_wait(met_sem, 1)
        for i, j in PLANE:
            signal(barrier, plane_peer(i, j)[1])
        for i in LINE:
            signal(barrier, z_peer((z + i) % NZ))
        signal(barrier, far_y)

    @pl.when(c == 0)
    def _():
        pl.semaphore_wait(barrier, 1)
        signal(met_sem, partner)

    for load in loads[:2]:
        load.wait()
    waves = wave_ref[...].astype(F32)
    kx = waves[0:1] * (4.0 / 1024.0)
    ky = waves[1:2] * (2.0 / 1024.0)
    kz = waves[2:3] * (1.0 / 1024.0)
    waves = rows16([kx, ky, kz, kx, ky, kz, 1.0], K)
    kv[...] = waves
    kt[...] = waves.T.astype(BF16)
    quarter = jnp.where(c == 0, 0.25, 0.0)

    def coords(px, py, pz, tile_z, shift):
        offsets = [(v * GRID).astype(F32) for v in (gx, gy, tile_z)]
        return rows16(
            [px.astype(F32), py.astype(F32), pz.astype(F32)] + offsets + [shift], TILE
        )

    for t in range(2):
        for i in range(3):
            halo_pos[17 + t, i] = pos_own[i, t : t + 1]

    def own_coords(shift):
        return [
            coords(*(halo_pos[17 + t, i] for i in range(3)), gz * 2 + t, shift)
            for t in range(2)
        ]

    own = own_coords(quarter)
    own_half = lanes(own).astype(BF16)
    other_half = lanes(own_coords(0.25 - quarter)).astype(BF16)
    for load in loads[2:4]:
        load.wait()
    own_feat = halo[17:19].reshape(2 * TILE, D)
    charge[...] = jnp.dot(own_feat, cw_ref[...], preferred_element_type=F32).astype(BF16)

    def factors(b, atoms):
        rows = pl.ds(pl.multiple_of(b * 128, 128), 128)
        cycles = jnp.dot(kt[rows], atoms, preferred_element_type=F32)
        table = sine_of_cycles(cycles).astype(BF16)
        return rows, jnp.dot(table, charge[...], preferred_element_type=F32)

    def group(i):
        return pl.multiple_of((gx + i) % NX * 256, 256)

    for i in ORDER:
        for h in range(2):
            rows, part = factors(group(i) // 128 + h, other_half)
            sx_send[rows] = part.astype(BF16)
    for i in ORDER:
        rows = pl.ds(group(i), 256)
        remote(
            sx_send.at[rows], sx_recv.at[rows], send_sem.at[2], sx_sem.at[i], partner
        ).start()

    for i in ORDER:
        for h in range(2):
            rows, part = factors(group(i) // 128 + h, own_half)
            s_own[rows] = part

    for i in ORDER:
        rows = pl.ds(group(i), 256)
        all_of(sx_recv.at[rows], sx_sem.at[i])
        both = s_own[rows] + sx_recv[rows].astype(F32)
        rs_send[pl.ds(group(i) // 64, 4)] = both.astype(BF16).reshape(4, 64, D)

    @pl.when(c == 1)
    def _():
        pl.semaphore_wait(barrier, 23)
        signal(met_sem, partner)

    @pl.when(c == 0)
    def _():
        pl.semaphore_wait(met_sem, 1)

    for i, j in PLANE:
        block, peer = plane_peer(i, j)
        remote(
            rs_send.at[block], rs_recv.at[q], coll_sem.at[0], coll_sem.at[1], peer
        ).start()

    def tiles(src, dst, n, sem, peer):
        return [
            remote(
                ref.at[pl.ds(src, n)], ref.at[pl.ds(dst, n)], send_sem.at[i], sem, peer
            )
            for i, ref in enumerate((halo, halo_pos))
        ]

    def got_tiles(n, sem):
        all_of(bytes_of.at[pl.ds(0, 67 * n)], sem)

    pair_copy = remote(
        halo_pos.at[pl.ds(17, 2)], pair_pos, send_sem.at[1], pair_sem, partner
    )

    def inner(col):
        return tiles(col * 4 + 2 - c, col * 4 + 3 * c, 1, hc_sem.at[col], partner)

    def sides(src, dst, end, sem, peer):
        if end:
            return tiles(src * 4 + 3 * c, dst * 4 + 3 * c, 1, sem, peer)
        return tiles(src * 4 + 1, dst * 4 + 1, 2, sem, peer)

    def to_y(up, end):
        col, peer = (3, gy_up) if up else (5, gy_down)
        return sides(4, col, end, hy_sem.at[end, up], peer)

    def to_x(up, k, end):
        peer = gx_up if up else gx_down
        dst = (0 if up else 6) + k
        return sides(3 + k, dst, end, hx_sem.at[end, 3 * up + k], peer)

    def start(copies):
        for copy in copies:
            copy.start()

    def got_y(up, end):
        got_tiles(2 - end, hy_sem.at[end, up])

    def got_x(up, k, end):
        got_tiles(2 - end, hx_sem.at[end, 3 * up + k])

    def got_inner(col):
        got_tiles(1, hc_sem.at[col])

    start(tiles(17 + c, 19 - 3 * c, 1, hz_sem, cross))
    pair_copy.start()
    for up in (1, 0):
        start(to_y(up, 0))
        start(to_x(up, 1, 0))
    start(inner(4))
    rs_recv[q] = rs_send[q]

    def all_but_one(buffer, n, sem):
        all_of(buffer.at[pl.ds(0, n - 1)], sem)

    def centre_rows(t):
        px = halo_pos[17 + t, 0] - 32
        py = halo_pos[17 + t, 1] - 32
        pz = halo_pos[17 + t, 2] + (GRID * t - 64)
        norm = px * px + py * py + pz * pz
        high = (norm >> 8) << 8
        scale = 1.0 / 64.0
        values = [-2 * px, -2 * py, -2 * pz, high, norm - high]
        values = [v.astype(F32) * scale for v in values]
        return rows16(values + [scale, scale], TILE)

    for t in range(2):
        targets[t] = centre_rows(t).T.astype(BF16)

    def radial_steps(col, slot):
        def squares():
            dx, dy = col // 3 - 1, col % 3 - 1
            at_ = [[halo_pos[col * 4 + s, i] for s in range(4)] for i in range(3)]
            px = lanes(at_[0]) + (dx * GRID - 32)
            py = lanes(at_[1]) + (dy * GRID - 32)
            pz = lanes([at_[2][s] + (GRID * s - 128) for s in range(4)])
            norm = px * px + py * py + pz * pz
            high = (norm >> 8) << 8
            scale = 1.0 / 64.0
            xs, ys, zs, hs, ls = (
                v.astype(F32) * scale for v in (px, py, pz, high, norm - high)
            )
            sources = rows16(
                [xs, ys, zs, scale, scale, hs, ls], 4 * TILE
            ).astype(BF16)
            for t in range(2):
                q2[slot, t] = jnp.dot(
                    targets[t],
                    sources[:, t * TILE : (t + 3) * TILE],
                    preferred_element_type=F32,
                )

        def some(t, part):
            rad = rads[slot * 2 + t]
            raw = q2[slot, t, part * 16 : part * 16 + 16]
            s2 = jnp.clip(raw, 1.0 / 8192.0, 1.0)
            s = s2 * lax.rsqrt(s2)
            rest = 1.0 - s2
            env = jnp.where(raw > 0.0, rest * rest, 0.0)
            step = jnp.exp2(s * (6.0 * LOG2E))
            value = env * jnp.exp2(s * (3.0 * LOG2E) - s2 * (18.0 * LOG2E))
            for r in range(NRBF):
                first = r * TILE + part * 16
                rad[first : first + 16] = value.astype(BF16)
                if r < NRBF - 1:
                    value = value * step

        return [squares] + [
            functools.partial(some, t, part) for t in range(2) for part in range(8)
        ]

    def pool_steps(col, slot, first=False):
        def some(t, r):
            near = halo[col * 4 + t : col * 4 + t + 3].reshape(3 * TILE, D)
            rows = slice(r * TILE, r * TILE + TILE)
            got = jnp.dot(rads[slot * 2 + t][rows], near, preferred_element_type=F32)
            if first:
                pool[t, rows] = got
            else:
                pool[t, rows] += got

        return [functools.partial(some, t, r) for t in range(2) for r in range(NRBF)]

    def weave(one, two):
        done = 0
        for i, step in enumerate(one):
            step()
            while done * len(one) < (i + 1) * len(two):
                two[done]()
                done += 1

    rads = (rad0, rad1, rad2, rad3)

    pair_copy.wait_recv()
    other = [
        coords(*(pair_pos[t, i] for i in range(3)), (gz + 1 - 2 * c) * 2 + t, quarter)
        for t in range(2)
    ]
    for t, tile in enumerate(own + other):
        ct[t * TILE : (t + 1) * TILE] = tile.T.astype(BF16)

    turned = []
    for i in range(4):
        part = kv[:, pl.ds(group(i), 256)]
        turned.append(pltpu.roll(part, (NY - y) % NY * 64, axis=1).astype(BF16))

    def table_block(b, carry):
        rows = pl.ds(pl.multiple_of(b * 64, 64), 64)
        for part in range(4):
            cols = slice(part * 256, part * 256 + 256)
            cycles = jnp.dot(ct[rows], turned[part], preferred_element_type=F32)
            tab_i[rows, cols] = sine_of_cycles(cycles).astype(BF16)
        return carry

    lax.fori_loop(0, 8, table_block, 0)

    got_tiles(1, hz_sem)
    for up in (1, 0):
        start(to_y(up, 1))
        start(to_x(up, 1, 1))

    got_inner(4)
    weave(radial_steps(4, 0), [])
    weave(pool_steps(4, 0, True), [])

    all_but_one(rs_recv, NX * NY, coll_sem.at[1])
    acc = rs_recv[0].astype(F32)
    for i in range(1, NX * NY):
        acc = acc + rs_recv[i].astype(F32)
    rz_send[...] = acc.astype(BF16)
    rz_recv[z] = rz_send[...]

    for i in LINE:
        remote(
            rz_send,
            rz_recv.at[z],
            coll_sem.at[2],
            coll_sem.at[3],
            z_peer((z + i) % NZ),
        ).start()

    for up, k in ((1, 0), (0, 2)):
        got_y(up, 0)
        start(inner(3 + k))
        start(to_x(1, k, 0))
        start(to_x(0, k, 0))
    for up, col in ((1, 1), (0, 7)):
        got_x(up, 1, 0)
        start(inner(col))
    for up, k in ((1, 0), (0, 2)):
        got_y(up, 1)
        start(to_x(1, k, 1))
        start(to_x(0, k, 1))
    got_inner(3)
    weave(radial_steps(3, 0), [])
    got_inner(5)
    weave(radial_steps(5, 1), pool_steps(3, 0))
    got_x(1, 1, 1)
    got_inner(1)
    weave(radial_steps(1, 0), pool_steps(5, 1))
    got_x(0, 1, 1)
    got_inner(7)
    weave(radial_steps(7, 1), pool_steps(1, 0))
    all_of(bytes_of, load_sem.at[4])
    mix_high = mix_ref[...].astype(BF16)
    mix_low = (mix_ref[...] - mix_high.astype(F32)).astype(BF16)

    all_but_one(rz_recv, NZ, coll_sem.at[3])
    total = rz_recv[0].astype(F32)
    for i in range(1, NZ):
        total = total + rz_recv[i].astype(F32)
    product = filt[...] * (total * (1.0 / 256.0))
    high = product.astype(BF16)
    low = (product - high.astype(F32)).astype(BF16)
    block = (
        jnp.dot(high, mix_high, preferred_element_type=F32)
        + jnp.dot(low, mix_high, preferred_element_type=F32)
        + jnp.dot(high, mix_low, preferred_element_type=F32)
    ).astype(BF16)
    ga_send[...] = block

    for i, j in PLANE:
        back = (4 - i) % 4
        remote(
            ga_send,
            ga_recv.at[back * 4 + (4 - j) % 4],
            coll_sem.at[4],
            ga_sem.at[back],
            plane_peer(i, j)[1],
        ).start()
    ga_recv[0] = block
    corners = ((1, 0, 0), (1, 2, 2), (0, 0, 6), (0, 2, 8))
    for up, k, col in corners:
        got_x(up, k, 0)
        start(inner(col))
    before = pool_steps(7, 1)
    for i, (up, k, col) in enumerate(corners):
        got_x(up, k, 1)
        got_inner(col)
        weave(radial_steps(col, i % 2), before)
        before = pool_steps(col, i % 2)
    weave(before, [])

    for t in range(2):
        message = jnp.zeros((TILE, D), F32)
        for r in range(NRBF):
            weight = math.exp(-18.0 * ((r + 0.5) / NRBF) ** 2)
            pooled = (pool[t, r * TILE : (r + 1) * TILE] * weight).astype(BF16)
            message = message + jnp.dot(
                pooled, rmix_ref[r * D : (r + 1) * D], preferred_element_type=F32
            )
        far[t * TILE : (t + 1) * TILE] = message + halo[17 + t].astype(F32)

    theirs = 0.0
    for i in (0, 1, 3, 2):
        some = ga_recv.at[pl.ds(i * 4, 4 if i else 3)]
        all_of(some, ga_sem.at[i])
        cols = slice(i * 256, i * 256 + 256)
        spectrum = ga_recv[i * 4 : i * 4 + 4].reshape(256, D)
        theirs = theirs + jnp.dot(
            tab_i[2 * TILE :, cols], spectrum, preferred_element_type=F32
        )
    ls_send[...] = theirs
    last = remote(ls_send, ls_recv, coll_sem.at[5], coll_sem.at[6], partner)
    last.start()
    ours = far[...] + jnp.dot(
        tab_i[: 2 * TILE], ga_recv[...].reshape(K, D), preferred_element_type=F32
    )
    last.wait_recv()
    summed = ours + ls_recv[...]
    mean = jnp.mean(summed * summed, axis=-1, keepdims=True)
    normed = summed * lax.rsqrt(mean + EPS) * gain_ref[...]
    hidden = jnp.dot(normed.astype(BF16), up_ref[...], preferred_element_type=F32)
    hidden = hidden / (1.0 + jnp.exp(-hidden))
    updated = summed + jnp.dot(
        hidden.astype(BF16), down_ref[...], preferred_element_type=F32
    )
    out_ref[...] = updated.astype(BF16).reshape(2, TILE, D)

    all_of(halo.at[pl.ds(0, 34)], send_sem.at[0])
    all_of(halo_pos, send_sem.at[1])
    all_of(sx_send, send_sem.at[2])
    all_but_one(rs_send, NX * NY, coll_sem.at[0])
    all_but_one(rz_recv, NZ, coll_sem.at[2])
    all_but_one(ga_recv, NX * NY, coll_sem.at[4])
    all_of(ls_send, coll_sem.at[5])


def on_device(features, positions, waves, rmix, cw, filters, mix, gain, up, down):
    feat = features.reshape(2, TILE, D)
    pos = positions.reshape(3, 2, TILE)
    hbm = pl.BlockSpec(memory_space=pl.ANY)
    dma = pltpu.SemaphoreType.DMA
    vmem = pltpu.VMEM
    out = pl.pallas_call(
        kernel,
        out_shape=pltpu.VMEM((2, TILE, D), BF16),
        in_specs=[hbm] * 10,
        out_specs=pl.BlockSpec(memory_space=pltpu.VMEM),
        scratch_shapes=[
            vmem((3, 2, TILE), jnp.int32),
            vmem((3, K), jnp.int32),
            vmem((D, D), BF16),
            vmem((64, D), F32),
            vmem((D, D), F32),
            vmem((NRBF * D, D), BF16),
            vmem((1, D), F32),
            vmem((D, 2 * D), BF16),
            vmem((2 * D, D), BF16),
            vmem((36, TILE, D), BF16),
            vmem((36, 3, 1, TILE), jnp.int32),
            vmem((2, 3, 1, TILE), jnp.int32),
            vmem((4 * TILE, K), BF16),
            vmem((K, D), BF16),
            vmem((K, D), BF16),
            vmem((K, D), F32),
            vmem((16, 64, D), BF16),
            vmem((16, 64, D), BF16),
            vmem((64, D), BF16),
            vmem((NZ, 64, D), BF16),
            vmem((64, D), BF16),
            vmem((16, 64, D), BF16),
            vmem((2 * TILE, D), F32),
            vmem((2 * TILE, D), F32),
            vmem((16, K), F32),
            vmem((K, 16), BF16),
            vmem((4 * TILE, 16), BF16),
            vmem((2 * TILE, D), BF16),
            vmem((2, 2, TILE, 3 * TILE), F32),
            vmem((2, TILE, 16), BF16),
            vmem((NRBF * TILE, 3 * TILE), BF16),
            vmem((NRBF * TILE, 3 * TILE), BF16),
            vmem((NRBF * TILE, 3 * TILE), BF16),
            vmem((NRBF * TILE, 3 * TILE), BF16),
            vmem((2, NRBF * TILE, D), F32),
            vmem((2 * TILE, D), F32),
            vmem((833, 1, D), F32),
            dma((5,)),
            dma((3,)),
            dma,
            dma,
            dma((2, 2)),
            dma((2, 6)),
            dma((9,)),
            dma((4,)),
            dma((7,)),
            dma((4,)),
            pltpu.SemaphoreType.REGULAR,
        ],
        compiler_params=pltpu.CompilerParams(collective_id=0, has_side_effects=True),
    )(feat, pos, waves, cw, filters, mix, rmix, gain.reshape(1, D), up, down)
    return out.reshape(features.shape)


def solution(mesh):
    tiles = P("gx", "gy", "gz", None, None)
    in_specs = (tiles, P(None, "gx", "gy", "gz", None)) + (P(),) * 8
    return jax.shard_map(
        on_device, mesh=mesh, in_specs=in_specs, out_specs=tiles, check_vma=False
    )
```

```python
import functools
import math

import jax
import jax.numpy as jnp
from jax import lax
from jax.experimental import pallas as pl
from jax.experimental.pallas import tpu as pltpu
from jax.sharding import PartitionSpec as P

MESH = pl.DeviceIdType.MESH
F32, BF16 = jnp.float32, jnp.bfloat16
NRBF = 6
GRID = 64
TILE = 128
D = 128
K = 1024
EPS = 1e-06
NX, NY, NZ = 4, 4, 8
LOG2E = 1.4426950408889634
ROUND = 12582912.0
SIN = (
    6.283182818518357,
    -41.341421396050286,
    81.5961838134782,
    -76.58009997779837,
    41.20539265997673,
    -12.271259128462068,
)
ORDER = (2, 1, 3, 0)
PLANE = [(i, j) for i in ORDER for j in ORDER if i or j]
INNER = (3, 2, 4, 1, 0, 1, 5, 2, 6)
LINE = sorted(range(1, 8), key=lambda i: -min(i, 8 - i))
FIRST = (((0,), (0,)), ((), ()))


def rows16(values, width):
    row = lax.broadcasted_iota(jnp.int32, (16, width), 0)
    out = jnp.zeros((16, width), F32)
    for at, value in enumerate(values):
        out = jnp.where(row == at, value, out)
    return out


def sine_of_cycles(cycles):
    f = cycles - ((cycles + ROUND) - ROUND)
    u = f * f
    acc = SIN[5]
    for c in SIN[4::-1]:
        acc = acc * u + c
    return acc * f


def lanes(tiles):
    return jnp.concatenate(tiles, axis=1)


def kernel(
    feat_hbm,
    pos_hbm,
    wave_hbm,
    cw_hbm,
    filt_hbm,
    mix_hbm,
    rmix_hbm,
    gain_hbm,
    up_hbm,
    down_hbm,
    out_ref,
    pos_own,
    wave_ref,
    cw_ref,
    filt,
    mix_ref,
    rmix_ref,
    gain_ref,
    up_ref,
    down_ref,
    halo,
    halo_pos,
    pair_pos,
    tab_i,
    sx_send,
    sx_recv,
    s_own,
    rs_send,
    rs_recv,
    rz_send,
    rz_recv,
    ga_send,
    ga_recv,
    ls_send,
    ls_recv,
    kv,
    kt,
    ct,
    charge,
    q2,
    targets,
    rad0,
    rad1,
    rad2,
    rad3,
    pool,
    far,
    bytes_of,
    load_sem,
    send_sem,
    pair_sem,
    hz_sem,
    hy_sem,
    hx_sem,
    hc_sem,
    sx_sem,
    coll_sem,
    ga_sem,
    met_sem,
):
    gx, gy, gz = lax.axis_index("gx"), lax.axis_index("gy"), lax.axis_index("gz")
    y, zl, zh, c = gy // 2, gy % 2, gz // 2, gz % 2
    z = zh * 2 + zl
    q = gx * NY + y

    def at(gx_, gy_, gz_):
        return {"gx": gx_, "gy": gy_, "gz": gz_}

    def plane_peer(i, j):
        x_, y_ = (gx + i) % NX, (y + j) % NY
        return x_ * NY + y_, at(x_, y_ * 2 + zl, gz)

    def z_peer(i):
        return at(gx, y * 2 + i % 2, (i // 2) * 2 + c)

    partner = at(gx, gy, gz + 1 - 2 * c)
    cross = at(gx, gy, (gz + 2 * c + 7) % 8)
    gy_up, gy_down = at(gx, (gy + 1) % 8, gz), at(gx, (gy + 7) % 8, gz)
    gx_up, gx_down = at((gx + 1) % 4, gy, gz), at((gx + 3) % 4, gy, gz)
    far_y = at(gx, (gy + 2 * zl + 7) % 8, gz)

    barrier = pltpu.get_barrier_semaphore()

    def signal(sem, peer):
        pl.semaphore_signal(sem, inc=1, device_id=peer, device_id_type=MESH)

    def remote(src, dst, send, recv, peer):
        return pltpu.make_async_remote_copy(
            src_ref=src,
            dst_ref=dst,
            send_sem=send,
            recv_sem=recv,
            device_id=peer,
            device_id_type=MESH,
        )

    def all_of(ref, sem):
        pltpu.make_async_copy(ref, ref, sem).wait()

    mine = pl.multiple_of(q * 64, 64)
    pairs = [
        (pos_hbm, pos_own),
        (wave_hbm, wave_ref),
        (feat_hbm, halo.at[pl.ds(17, 2)]),
        (cw_hbm, cw_ref),
        (filt_hbm.at[pl.ds(mine, 64)], filt),
        (mix_hbm, mix_ref),
        (rmix_hbm, rmix_ref),
        (gain_hbm, gain_ref),
        (up_hbm, up_ref),
        (down_hbm, down_ref),
    ]
    loads = [
        pltpu.make_async_copy(src, dst, load_sem.at[min(i, 4)])
        for i, (src, dst) in enumerate(pairs)
    ]
    for load in loads[:4]:
        load.start()

    for load in loads[4:]:
        load.start()

    @pl.when(c == 1)
    def _():
        signal(barrier, partner)
        pl.semaphore_wait(met_sem, 1)
        for i, j in PLANE:
            signal(barrier, plane_peer(i, j)[1])
        for i in LINE:
            signal(barrier, z_peer((z + i) % NZ))
        signal(barrier, far_y)

    @pl.when(c == 0)
    def _():
        pl.semaphore_wait(barrier, 1)
        signal(met_sem, partner)

    for load in loads[:2]:
        load.wait()
    waves = wave_ref[...].astype(F32)
    kx = waves[0:1] * (4.0 / 1024.0)
    ky = waves[1:2] * (2.0 / 1024.0)
    kz = waves[2:3] * (1.0 / 1024.0)
    waves = rows16([kx, ky, kz, kx, ky, kz, 1.0], K)
    kv[...] = waves
    kt[...] = waves.T.astype(BF16)
    quarter = jnp.where(c == 0, 0.25, 0.0)

    def coords(px, py, pz, tile_z, shift):
        offsets = [(v * GRID).astype(F32) for v in (gx, gy, tile_z)]
        return rows16(
            [px.astype(F32), py.astype(F32), pz.astype(F32)] + offsets + [shift], TILE
        )

    for t in range(2):
        for i in range(3):
            halo_pos[17 + t, i] = pos_own[i, t : t + 1]

    def own_coords(shift):
        return [
            coords(*(halo_pos[17 + t, i] for i in range(3)), gz * 2 + t, shift)
            for t in range(2)
        ]

    own = own_coords(quarter)
    own_half = lanes(own).astype(BF16)
    other_half = lanes(own_coords(0.25 - quarter)).astype(BF16)
    for load in loads[2:4]:
        load.wait()
    own_feat = halo[17:19].reshape(2 * TILE, D)
    charge[...] = jnp.dot(own_feat, cw_ref[...], preferred_element_type=F32).astype(BF16)

    def factors(b, atoms):
        rows = pl.ds(pl.multiple_of(b * 128, 128), 128)
        cycles = jnp.dot(kt[rows], atoms, preferred_element_type=F32)
        table = sine_of_cycles(cycles).astype(BF16)
        return rows, jnp.dot(table, charge[...], preferred_element_type=F32)

    def group(i):
        return pl.multiple_of((gx + i) % NX * 256, 256)

    for i in ORDER:
        for h in range(2):
            rows, part = factors(group(i) // 128 + h, other_half)
            sx_send[rows] = part.astype(BF16)
    for i in ORDER:
        rows = pl.ds(group(i), 256)
        remote(
            sx_send.at[rows], sx_recv.at[rows], send_sem.at[2], sx_sem, partner
        ).start()

    for i in ORDER:
        for h in range(2):
            rows, part = factors(group(i) // 128 + h, own_half)
            s_own[rows] = part

    all_of(sx_recv, sx_sem)
    for i in ORDER:
        rows = pl.ds(group(i), 256)
        both = s_own[rows] + sx_recv[rows].astype(F32)
        rs_send[pl.ds(group(i) // 64, 4)] = both.astype(BF16).reshape(4, 64, D)

    @pl.when(c == 1)
    def _():
        pl.semaphore_wait(barrier, 23)
        signal(met_sem, partner)

    @pl.when(c == 0)
    def _():
        pl.semaphore_wait(met_sem, 1)

    for i, j in PLANE:
        block, peer = plane_peer(i, j)
        remote(
            rs_send.at[block], rs_recv.at[q], coll_sem.at[0], coll_sem.at[1], peer
        ).start()

    def tiles(src, dst, n, sem, peer):
        return [
            remote(
                ref.at[pl.ds(src, n)], ref.at[pl.ds(dst, n)], send_sem.at[i], sem, peer
            )
            for i, ref in enumerate((halo, halo_pos))
        ]

    def got_tiles(n, sem):
        all_of(bytes_of.at[pl.ds(0, 67 * n)], sem)

    pair_copy = remote(
        halo_pos.at[pl.ds(17, 2)], pair_pos, send_sem.at[1], pair_sem, partner
    )

    def inner(col):
        return tiles(col * 4 + 2 - c, col * 4 + 3 * c, 1, hc_sem.at[INNER[col]], partner)

    def sides(src, dst, end, sem, peer):
        if end:
            return tiles(src * 4 + 3 * c, dst * 4 + 3 * c, 1, sem, peer)
        return tiles(src * 4 + 1, dst * 4 + 1, 2, sem, peer)

    def to_y(up, end):
        col, peer = (3, gy_up) if up else (5, gy_down)
        return sides(4, col, end, hy_sem.at[2 * end + (0 if end else up)], peer)

    def to_x(up, k, end):
        peer = gx_up if up else gx_down
        dst = (0 if up else 6) + k
        return sides(3 + k, dst, end, hx_sem.at[end, 4 if k == 1 else 2 * up + k // 2], peer)

    def start(copies):
        for copy in copies:
            copy.start()

    def got_y_own(up):
        got_tiles(2, hy_sem.at[up])

    def got_y_ends():
        got_tiles(2, hy_sem.at[2])

    def got_x_middle(end):
        got_tiles(2 * (2 - end), hx_sem.at[end, 4])

    def got_x(up, k, end):
        got_tiles(2 - end, hx_sem.at[end, 2 * up + k // 2])

    def got_inner(col):
        got_tiles(INNER.count(INNER[col]), hc_sem.at[INNER[col]])

    start(tiles(17 + c, 19 - 3 * c, 1, hz_sem, cross))
    pair_copy.start()
    for up in (1, 0):

        @pl.when(zl != up)
        def _():
            start(to_y(up, 0))

    for up in (1, 0):
        start(to_x(up, 1, 0))
    start(inner(4))
    rs_recv[q] = rs_send[q]

    def all_but_one(buffer, n, sem):
        all_of(buffer.at[pl.ds(0, n - 1)], sem)

    def centre_rows(t):
        px = halo_pos[17 + t, 0] - 32
        py = halo_pos[17 + t, 1] - 32
        pz = halo_pos[17 + t, 2] + (GRID * t - 64)
        norm = px * px + py * py + pz * pz
        high = (norm >> 8) << 8
        scale = 1.0 / 64.0
        values = [-2 * px, -2 * py, -2 * pz, high, norm - high]
        values = [v.astype(F32) * scale for v in values]
        return rows16(values + [scale, scale], TILE)

    for t in range(2):
        targets[t] = centre_rows(t).T.astype(BF16)

    def radial_steps(col, slot):
        def squares():
            dx, dy = col // 3 - 1, col % 3 - 1
            at_ = [[halo_pos[col * 4 + s, i] for s in range(4)] for i in range(3)]
            px = lanes(at_[0]) + (dx * GRID - 32)
            py = lanes(at_[1]) + (dy * GRID - 32)
            pz = lanes([at_[2][s] + (GRID * s - 128) for s in range(4)])
            norm = px * px + py * py + pz * pz
            high = (norm >> 8) << 8
            scale = 1.0 / 64.0
            xs, ys, zs, hs, ls = (
                v.astype(F32) * scale for v in (px, py, pz, high, norm - high)
            )
            sources = rows16(
                [xs, ys, zs, scale, scale, hs, ls], 4 * TILE
            ).astype(BF16)
            for t in range(2):
                q2[slot, t] = jnp.dot(
                    targets[t],
                    sources[:, t * TILE : (t + 3) * TILE],
                    preferred_element_type=F32,
                )

        def some(t, part):
            rad = rads[slot * 2 + t]
            raw = q2[slot, t, part * 16 : part * 16 + 16]
            s2 = jnp.clip(raw, 1.0 / 8192.0, 1.0)
            s = s2 * lax.rsqrt(s2)
            rest = 1.0 - s2
            env = jnp.where(raw > 0.0, rest * rest, 0.0)
            step = jnp.exp2(s * (6.0 * LOG2E))
            value = env * jnp.exp2(s * (3.0 * LOG2E) - s2 * (18.0 * LOG2E))
            for r in range(NRBF):
                first = r * TILE + part * 16
                rad[first : first + 16] = value.astype(BF16)
                if r < NRBF - 1:
                    value = value * step

        return [squares] + [
            functools.partial(some, t, part) for t in range(2) for part in range(8)
        ]

    def pool_steps(col, slot, first=False):
        def some(t, r):
            near = halo[col * 4 + t : col * 4 + t + 3].reshape(3 * TILE, D)
            rows = slice(r * TILE, r * TILE + TILE)
            got = jnp.dot(rads[slot * 2 + t][rows], near, preferred_element_type=F32)
            if first:
                pool[t, rows] = got
            else:
                pool[t, rows] += got

        return [functools.partial(some, t, r) for t in range(2) for r in range(NRBF)]

    def weave(one, two):
        done = 0
        for i, step in enumerate(one or [lambda: None]):
            step()
            while done * max(len(one), 1) < (i + 1) * len(two):
                two[done]()
                done += 1

    rads = (rad0, rad1, rad2, rad3)

    pair_copy.wait_recv()
    other = [
        coords(*(pair_pos[t, i] for i in range(3)), (gz + 1 - 2 * c) * 2 + t, quarter)
        for t in range(2)
    ]
    for t, tile in enumerate(own + other):
        ct[t * TILE : (t + 1) * TILE] = tile.T.astype(BF16)

    turned = []
    for i in range(4):
        part = kv[:, pl.ds(group(i), 256)]
        turned.append(pltpu.roll(part, (NY - y) % NY * 64, axis=1).astype(BF16))

    def table_block(b, carry):
        rows = pl.ds(pl.multiple_of(b * 64, 64), 64)
        for part in range(4):
            cols = slice(part * 256, part * 256 + 256)
            cycles = jnp.dot(ct[rows], turned[part], preferred_element_type=F32)
            tab_i[rows, cols] = sine_of_cycles(cycles).astype(BF16)
        return carry

    lax.fori_loop(0, 4, table_block, 0)
    for up in (1, 0):

        @pl.when(zl == up)
        def _():
            start(to_y(up, 0))

    lax.fori_loop(4, 8, table_block, 0)

    got_tiles(1, hz_sem)
    for up in (1, 0):
        start(to_y(up, 1))
        start(to_x(up, 1, 1))

    got_inner(4)
    weave(radial_steps(4, 0), [])
    weave(pool_steps(4, 0, True), [])

    all_but_one(rs_recv, NX * NY, coll_sem.at[1])
    acc = rs_recv[0].astype(F32)
    for i in range(1, NX * NY):
        acc = acc + rs_recv[i].astype(F32)
    rz_send[...] = acc.astype(BF16)
    rz_recv[z] = rz_send[...]

    for i in LINE:
        remote(
            rz_send,
            rz_recv.at[z],
            coll_sem.at[2],
            coll_sem.at[3],
            z_peer((z + i) % NZ),
        ).start()

    def onward(near):
        for up, k in ((1, 0), (0, 2)):

            @pl.when((zl == up) == near)
            def _():
                got_y_own(up)
                start(inner(3 + k))
                start(to_x(1, k, 0))
                start(to_x(0, k, 0))

    onward(True)
    got_x_middle(0)
    for col in (1, 7):
        start(inner(col))
    onward(False)
    got_x_middle(1)
    got_inner(1)
    weave(radial_steps(1, 0), [])
    weave(radial_steps(7, 1), pool_steps(1, 0))
    got_y_ends()
    for k in (0, 2):
        start(to_x(1, k, 1))
        start(to_x(0, k, 1))
    got_inner(3)
    weave(radial_steps(3, 0), pool_steps(7, 1))
    weave(radial_steps(5, 1), pool_steps(3, 0))
    all_of(bytes_of, load_sem.at[4])
    mix_high = mix_ref[...].astype(BF16)
    mix_low = (mix_ref[...] - mix_high.astype(F32)).astype(BF16)

    all_but_one(rz_recv, NZ, coll_sem.at[3])
    total = rz_recv[0].astype(F32)
    for i in range(1, NZ):
        total = total + rz_recv[i].astype(F32)
    product = filt[...] * (total * (1.0 / 256.0))
    high = product.astype(BF16)
    low = (product - high.astype(F32)).astype(BF16)
    block = (
        jnp.dot(high, mix_high, preferred_element_type=F32)
        + jnp.dot(low, mix_high, preferred_element_type=F32)
        + jnp.dot(high, mix_low, preferred_element_type=F32)
    ).astype(BF16)
    ga_send[...] = block

    for i, j in PLANE:
        back = (4 - i) % 4
        remote(
            ga_send,
            ga_recv.at[back * 4 + (4 - j) % 4],
            coll_sem.at[4],
            ga_sem.at[back],
            plane_peer(i, j)[1],
        ).start()
    ga_recv[0] = block
    corners = ((1, 0, 0), (1, 2, 2), (0, 0, 6), (0, 2, 8))
    for up, k, col in corners:
        got_x(up, k, 0)
        start(inner(col))
    before = pool_steps(5, 1)
    for i, (up, k, col) in enumerate(corners):
        got_x(up, k, 1)
        got_inner(col)
        weave(radial_steps(col, i % 2), before)
        before = pool_steps(col, i % 2)
    weave(before, [])

    for t in range(2):
        message = jnp.zeros((TILE, D), F32)
        for r in range(NRBF):
            weight = math.exp(-18.0 * ((r + 0.5) / NRBF) ** 2)
            pooled = (pool[t, r * TILE : (r + 1) * TILE] * weight).astype(BF16)
            message = message + jnp.dot(
                pooled, rmix_ref[r * D : (r + 1) * D], preferred_element_type=F32
            )
        far[t * TILE : (t + 1) * TILE] = message + halo[17 + t].astype(F32)

    theirs = 0.0
    for i in (0, 1, 3, 2):
        some = ga_recv.at[pl.ds(i * 4, 4 if i else 3)]
        all_of(some, ga_sem.at[i])
        theirs = theirs + jnp.dot(
            tab_i[2 * TILE :, i * 256 : i * 256 + 256],
            ga_recv[i * 4 : i * 4 + 4].reshape(256, D),
            preferred_element_type=F32,
        )
    ls_send[...] = theirs.astype(BF16)
    last = remote(ls_send, ls_recv, coll_sem.at[5], coll_sem.at[6], partner)
    last.start()
    ours = far[...] + jnp.dot(
        tab_i[: 2 * TILE], ga_recv[...].reshape(K, D), preferred_element_type=F32
    )
    last.wait_recv()
    summed = ours + ls_recv[...].astype(F32)
    mean = jnp.mean(summed * summed, axis=-1, keepdims=True)
    normed = summed * lax.rsqrt(mean + EPS) * gain_ref[...]
    hidden = jnp.dot(normed.astype(BF16), up_ref[...], preferred_element_type=F32)
    hidden = hidden / (1.0 + jnp.exp(-hidden))
    updated = summed + jnp.dot(
        hidden.astype(BF16), down_ref[...], preferred_element_type=F32
    )
    out_ref[...] = updated.astype(BF16).reshape(2, TILE, D)

    all_of(halo.at[pl.ds(0, 34)], send_sem.at[0])
    all_of(halo_pos, send_sem.at[1])
    all_of(sx_send, send_sem.at[2])
    all_but_one(rs_send, NX * NY, coll_sem.at[0])
    all_but_one(rz_recv, NZ, coll_sem.at[2])
    all_but_one(ga_recv, NX * NY, coll_sem.at[4])
    all_of(ls_send, coll_sem.at[5])


def on_device(features, positions, waves, rmix, cw, filters, mix, gain, up, down):
    feat = features.reshape(2, TILE, D)
    pos = positions.reshape(3, 2, TILE)
    hbm = pl.BlockSpec(memory_space=pl.ANY)
    dma = pltpu.SemaphoreType.DMA
    vmem = pltpu.VMEM
    out = pl.pallas_call(
        kernel,
        out_shape=pltpu.VMEM((2, TILE, D), BF16),
        in_specs=[hbm] * 10,
        out_specs=pl.BlockSpec(memory_space=pltpu.VMEM),
        scratch_shapes=[
            vmem((3, 2, TILE), jnp.int32),
            vmem((3, K), jnp.int32),
            vmem((D, D), BF16),
            vmem((64, D), F32),
            vmem((D, D), F32),
            vmem((NRBF * D, D), BF16),
            vmem((1, D), F32),
            vmem((D, 2 * D), BF16),
            vmem((2 * D, D), BF16),
            vmem((36, TILE, D), BF16),
            vmem((36, 3, 1, TILE), jnp.int32),
            vmem((2, 3, 1, TILE), jnp.int32),
            vmem((4 * TILE, K), BF16),
            vmem((K, D), BF16),
            vmem((K, D), BF16),
            vmem((K, D), F32),
            vmem((16, 64, D), BF16),
            vmem((16, 64, D), BF16),
            vmem((64, D), BF16),
            vmem((NZ, 64, D), BF16),
            vmem((64, D), BF16),
            vmem((16, 64, D), BF16),
            vmem((2 * TILE, D), BF16),
            vmem((2 * TILE, D), BF16),
            vmem((16, K), F32),
            vmem((K, 16), BF16),
            vmem((4 * TILE, 16), BF16),
            vmem((2 * TILE, D), BF16),
            vmem((2, 2, TILE, 3 * TILE), F32),
            vmem((2, TILE, 16), BF16),
            vmem((NRBF * TILE, 3 * TILE), BF16),
            vmem((NRBF * TILE, 3 * TILE), BF16),
            vmem((NRBF * TILE, 3 * TILE), BF16),
            vmem((NRBF * TILE, 3 * TILE), BF16),
            vmem((2, NRBF * TILE, D), F32),
            vmem((2 * TILE, D), F32),
            vmem((833, 1, D), F32),
            dma((5,)),
            dma((3,)),
            dma,
            dma,
            dma((3,)),
            dma((2, 5)),
            dma((7,)),
            dma,
            dma((7,)),
            dma((4,)),
            pltpu.SemaphoreType.REGULAR,
        ],
        compiler_params=pltpu.CompilerParams(collective_id=0, has_side_effects=True),
    )(feat, pos, waves, cw, filters, mix, rmix, gain.reshape(1, D), up, down)
    return out.reshape(features.shape)


def solution(mesh):
    tiles = P("gx", "gy", "gz", None, None)
    in_specs = (tiles, P(None, "gx", "gy", "gz", None)) + (P(),) * 8
    return jax.shard_map(
        on_device, mesh=mesh, in_specs=in_specs, out_specs=tiles, check_vma=False
    )
```

```python
import functools
import math

import jax
import jax.numpy as jnp
from jax import lax
from jax.experimental import pallas as pl
from jax.experimental.pallas import tpu as pltpu
from jax.sharding import PartitionSpec as P

MESH = pl.DeviceIdType.MESH
F32, BF16 = jnp.float32, jnp.bfloat16
NRBF = 6
GRID = 64
TILE = 128
D = 128
K = 1024
EPS = 1e-06
NX, NY, NZ = 4, 4, 8
LOG2E = 1.4426950408889634
ROUND = 12582912.0
SIN = (
    6.283182818518357,
    -41.341421396050286,
    81.5961838134782,
    -76.58009997779837,
    41.20539265997673,
    -12.271259128462068,
)
ORDER = (2, 1, 3, 0)
ALONG = [(i, j) for i in (2, 1) for j in ORDER]
BACK = [(3, 2), (0, 2), (3, 1), (0, 1), (3, 3), (0, 3), (3, 0)]
PLANE = [step for pair in zip(ALONG, BACK) for step in pair] + ALONG[7:]
INNER = (3, 2, 4, 1, 0, 1, 5, 2, 6)
LINE = sorted(range(1, 8), key=lambda i: -min(i, 8 - i))
FIRST = (((0,), (0,)), ((), ()))


def rows16(values, width):
    row = lax.broadcasted_iota(jnp.int32, (16, width), 0)
    out = jnp.zeros((16, width), F32)
    for at, value in enumerate(values):
        out = jnp.where(row == at, value, out)
    return out


def sine_of_cycles(cycles):
    f = cycles - ((cycles + ROUND) - ROUND)
    u = f * f
    acc = SIN[5]
    for c in SIN[4::-1]:
        acc = acc * u + c
    return acc * f


def lanes(tiles):
    return jnp.concatenate(tiles, axis=1)


def kernel(
    feat_hbm,
    pos_hbm,
    wave_hbm,
    cw_hbm,
    filt_hbm,
    mix_hbm,
    rmix_hbm,
    gain_hbm,
    up_hbm,
    down_hbm,
    out_ref,
    pos_own,
    wave_ref,
    cw_ref,
    filt,
    mix_ref,
    rmix_ref,
    gain_ref,
    up_ref,
    down_ref,
    halo,
    halo_pos,
    pair_pos,
    tab_i,
    sx_send,
    sx_recv,
    s_own,
    rs_send,
    rs_recv,
    rz_send,
    rz_recv,
    ga_send,
    ga_recv,
    ls_send,
    ls_recv,
    kv,
    kt,
    ct,
    charge,
    q2,
    targets,
    rad0,
    rad1,
    rad2,
    rad3,
    pool,
    far,
    bytes_of,
    load_sem,
    send_sem,
    pair_sem,
    hz_sem,
    hy_sem,
    hx_sem,
    hc_sem,
    sx_sem,
    coll_sem,
    ga_sem,
    met_sem,
):
    gx, gy, gz = lax.axis_index("gx"), lax.axis_index("gy"), lax.axis_index("gz")
    y, zl, zh, c = gy // 2, gy % 2, gz // 2, gz % 2
    z = zh * 2 + zl
    q = gx * NY + y

    def at(gx_, gy_, gz_):
        return {"gx": gx_, "gy": gy_, "gz": gz_}

    def plane_peer(i, j):
        x_, y_ = (gx + i) % NX, (y + j) % NY
        return x_ * NY + y_, at(x_, y_ * 2 + zl, gz)

    def z_peer(i):
        return at(gx, y * 2 + i % 2, (i // 2) * 2 + c)

    partner = at(gx, gy, gz + 1 - 2 * c)
    cross = at(gx, gy, (gz + 2 * c + 7) % 8)
    gy_up, gy_down = at(gx, (gy + 1) % 8, gz), at(gx, (gy + 7) % 8, gz)
    gx_up, gx_down = at((gx + 1) % 4, gy, gz), at((gx + 3) % 4, gy, gz)
    far_y = at(gx, (gy + 2 * zl + 7) % 8, gz)

    barrier = pltpu.get_barrier_semaphore()

    def signal(sem, peer):
        pl.semaphore_signal(sem, inc=1, device_id=peer, device_id_type=MESH)

    def remote(src, dst, send, recv, peer):
        return pltpu.make_async_remote_copy(
            src_ref=src,
            dst_ref=dst,
            send_sem=send,
            recv_sem=recv,
            device_id=peer,
            device_id_type=MESH,
        )

    def all_of(ref, sem):
        pltpu.make_async_copy(ref, ref, sem).wait()

    mine = pl.multiple_of(q * 64, 64)
    pairs = [
        (pos_hbm, pos_own),
        (wave_hbm, wave_ref),
        (feat_hbm, halo.at[pl.ds(17, 2)]),
        (cw_hbm, cw_ref),
        (filt_hbm.at[pl.ds(mine, 64)], filt),
        (mix_hbm, mix_ref),
        (rmix_hbm, rmix_ref),
        (gain_hbm, gain_ref),
        (up_hbm, up_ref),
        (down_hbm, down_ref),
    ]
    loads = [
        pltpu.make_async_copy(src, dst, load_sem.at[min(i, 4)])
        for i, (src, dst) in enumerate(pairs)
    ]
    for load in loads[:4]:
        load.start()

    for load in loads[4:]:
        load.start()

    @pl.when(c == 1)
    def _():
        signal(barrier, partner)
        pl.semaphore_wait(met_sem, 1)
        for i, j in PLANE:
            signal(barrier, plane_peer(i, j)[1])
        for i in LINE:
            signal(barrier, z_peer((z + i) % NZ))
        signal(barrier, far_y)

    @pl.when(c == 0)
    def _():
        pl.semaphore_wait(barrier, 1)
        signal(met_sem, partner)

    for load in loads[:2]:
        load.wait()
    waves = wave_ref[...].astype(F32)
    kx = waves[0:1] * (4.0 / 1024.0)
    ky = waves[1:2] * (2.0 / 1024.0)
    kz = waves[2:3] * (1.0 / 1024.0)
    waves = rows16([kx, ky, kz, kx, ky, kz, 1.0], K)
    kv[...] = waves
    kt[...] = waves.T.astype(BF16)
    quarter = jnp.where(c == 0, 0.25, 0.0)

    def coords(px, py, pz, tile_z, shift):
        offsets = [(v * GRID).astype(F32) for v in (gx, gy, tile_z)]
        return rows16(
            [px.astype(F32), py.astype(F32), pz.astype(F32)] + offsets + [shift], TILE
        )

    for t in range(2):
        for i in range(3):
            halo_pos[17 + t, i] = pos_own[i, t : t + 1]

    def own_coords(shift):
        return [
            coords(*(halo_pos[17 + t, i] for i in range(3)), gz * 2 + t, shift)
            for t in range(2)
        ]

    own = own_coords(quarter)
    own_half = lanes(own).astype(BF16)
    other_half = lanes(own_coords(0.25 - quarter)).astype(BF16)
    for load in loads[2:4]:
        load.wait()
    own_feat = halo[17:19].reshape(2 * TILE, D)
    charge[...] = jnp.dot(own_feat, cw_ref[...], preferred_element_type=F32).astype(BF16)

    def factors(b, atoms):
        rows = pl.ds(pl.multiple_of(b * 128, 128), 128)
        cycles = jnp.dot(kt[rows], atoms, preferred_element_type=F32)
        table = sine_of_cycles(cycles).astype(BF16)
        return rows, jnp.dot(table, charge[...], preferred_element_type=F32)

    def group(i):
        return pl.multiple_of((gx + i) % NX * 256, 256)

    for i in ORDER:
        for h in range(2):
            rows, part = factors(group(i) // 128 + h, other_half)
            sx_send[rows] = part.astype(BF16)
    for i in ORDER:
        rows = pl.ds(group(i), 256)
        remote(
            sx_send.at[rows], sx_recv.at[rows], send_sem.at[2], sx_sem, partner
        ).start()

    for i in ORDER:
        for h in range(2):
            rows, part = factors(group(i) // 128 + h, own_half)
            s_own[rows] = part

    all_of(sx_recv, sx_sem)
    for i in ORDER:
        rows = pl.ds(group(i), 256)
        both = s_own[rows] + sx_recv[rows].astype(F32)
        rs_send[pl.ds(group(i) // 64, 4)] = both.astype(BF16).reshape(4, 64, D)

    @pl.when(c == 1)
    def _():
        pl.semaphore_wait(barrier, 23)
        signal(met_sem, partner)

    @pl.when(c == 0)
    def _():
        pl.semaphore_wait(met_sem, 1)

    for i, j in PLANE:
        block, peer = plane_peer(i, j)
        remote(
            rs_send.at[block], rs_recv.at[q], coll_sem.at[0], coll_sem.at[1], peer
        ).start()

    def tiles(src, dst, n, sem, peer):
        return [
            remote(
                ref.at[pl.ds(src, n)], ref.at[pl.ds(dst, n)], send_sem.at[i], sem, peer
            )
            for i, ref in enumerate((halo, halo_pos))
        ]

    def got_tiles(n, sem):
        all_of(bytes_of.at[pl.ds(0, 67 * n)], sem)

    pair_copy = remote(
        halo_pos.at[pl.ds(17, 2)], pair_pos, send_sem.at[1], pair_sem, partner
    )

    def inner(col):
        return tiles(col * 4 + 2 - c, col * 4 + 3 * c, 1, hc_sem.at[INNER[col]], partner)

    def sides(src, dst, end, sem, peer):
        if end:
            return tiles(src * 4 + 3 * c, dst * 4 + 3 * c, 1, sem, peer)
        return tiles(src * 4 + 1, dst * 4 + 1, 2, sem, peer)

    def to_y(up, end):
        col, peer = (3, gy_up) if up else (5, gy_down)
        return sides(4, col, end, hy_sem.at[2 * end + (0 if end else up)], peer)

    def to_x(up, k, end):
        peer = gx_up if up else gx_down
        dst = (0 if up else 6) + k
        return sides(3 + k, dst, end, hx_sem.at[end, 4 if k == 1 else 2 * up + k // 2], peer)

    def start(copies):
        for copy in copies:
            copy.start()

    def got_y_own(up):
        got_tiles(2, hy_sem.at[up])

    def got_y_ends():
        got_tiles(2, hy_sem.at[2])

    def got_x_middle(end):
        got_tiles(2 * (2 - end), hx_sem.at[end, 4])

    def got_x(up, k, end):
        got_tiles(2 - end, hx_sem.at[end, 2 * up + k // 2])

    def got_inner(col):
        got_tiles(INNER.count(INNER[col]), hc_sem.at[INNER[col]])

    start(tiles(17 + c, 19 - 3 * c, 1, hz_sem, cross))
    pair_copy.start()
    for up in (1, 0):

        @pl.when(zl != up)
        def _():
            start(to_y(up, 0))

    start(inner(4))
    rs_recv[q] = rs_send[q]

    def all_but_one(buffer, n, sem):
        all_of(buffer.at[pl.ds(0, n - 1)], sem)

    def centre_rows(t):
        px = halo_pos[17 + t, 0] - 32
        py = halo_pos[17 + t, 1] - 32
        pz = halo_pos[17 + t, 2] + (GRID * t - 64)
        norm = px * px + py * py + pz * pz
        high = (norm >> 8) << 8
        scale = 1.0 / 64.0
        values = [-2 * px, -2 * py, -2 * pz, high, norm - high]
        values = [v.astype(F32) * scale for v in values]
        return rows16(values + [scale, scale], TILE)

    for t in range(2):
        targets[t] = centre_rows(t).T.astype(BF16)

    def radial_steps(col, slot):
        def squares():
            dx, dy = col // 3 - 1, col % 3 - 1
            at_ = [[halo_pos[col * 4 + s, i] for s in range(4)] for i in range(3)]
            px = lanes(at_[0]) + (dx * GRID - 32)
            py = lanes(at_[1]) + (dy * GRID - 32)
            pz = lanes([at_[2][s] + (GRID * s - 128) for s in range(4)])
            norm = px * px + py * py + pz * pz
            high = (norm >> 8) << 8
            scale = 1.0 / 64.0
            xs, ys, zs, hs, ls = (
                v.astype(F32) * scale for v in (px, py, pz, high, norm - high)
            )
            sources = rows16(
                [xs, ys, zs, scale, scale, hs, ls], 4 * TILE
            ).astype(BF16)
            for t in range(2):
                q2[slot, t] = jnp.dot(
                    targets[t],
                    sources[:, t * TILE : (t + 3) * TILE],
                    preferred_element_type=F32,
                )

        def some(t, part):
            rad = rads[slot * 2 + t]
            raw = q2[slot, t, part * 16 : part * 16 + 16]
            s2 = jnp.clip(raw, 1.0 / 8192.0, 1.0)
            s = s2 * lax.rsqrt(s2)
            rest = 1.0 - s2
            env = jnp.where(raw > 0.0, rest * rest, 0.0)
            step = jnp.exp2(s * (6.0 * LOG2E))
            value = env * jnp.exp2(s * (3.0 * LOG2E) - s2 * (18.0 * LOG2E))
            for r in range(NRBF):
                first = r * TILE + part * 16
                rad[first : first + 16] = value.astype(BF16)
                if r < NRBF - 1:
                    value = value * step

        return [squares] + [
            functools.partial(some, t, part) for t in range(2) for part in range(8)
        ]

    def pool_steps(col, slot, first=False):
        def some(t, r):
            near = halo[col * 4 + t : col * 4 + t + 3].reshape(3 * TILE, D)
            rows = slice(r * TILE, r * TILE + TILE)
            got = jnp.dot(rads[slot * 2 + t][rows], near, preferred_element_type=F32)
            if first:
                pool[t, rows] = got
            else:
                pool[t, rows] += got

        return [functools.partial(some, t, r) for t in range(2) for r in range(NRBF)]

    def weave(one, two):
        done = 0
        for i, step in enumerate(one or [lambda: None]):
            step()
            while done * max(len(one), 1) < (i + 1) * len(two):
                two[done]()
                done += 1

    rads = (rad0, rad1, rad2, rad3)

    pair_copy.wait_recv()
    other = [
        coords(*(pair_pos[t, i] for i in range(3)), (gz + 1 - 2 * c) * 2 + t, quarter)
        for t in range(2)
    ]
    for t, tile in enumerate(own + other):
        ct[t * TILE : (t + 1) * TILE] = tile.T.astype(BF16)

    turned = []
    for i in range(4):
        part = kv[:, pl.ds(group(i), 256)]
        turned.append(pltpu.roll(part, (NY - y) % NY * 64, axis=1).astype(BF16))

    def table_block(b, carry):
        rows = pl.ds(pl.multiple_of(b * 64, 64), 64)
        for part in range(4):
            cols = slice(part * 256, part * 256 + 256)
            cycles = jnp.dot(ct[rows], turned[part], preferred_element_type=F32)
            tab_i[rows, cols] = sine_of_cycles(cycles).astype(BF16)
        return carry

    lax.fori_loop(0, 4, table_block, 0)
    for up in (1, 0):

        @pl.when(zl == up)
        def _():
            start(to_y(up, 0))

    for up in (1, 0):
        start(to_x(up, 1, 0))
    lax.fori_loop(4, 8, table_block, 0)

    got_tiles(1, hz_sem)
    for up in (1, 0):
        start(to_y(up, 1))
        start(to_x(up, 1, 1))

    got_inner(4)
    weave(radial_steps(4, 0), [])
    weave(pool_steps(4, 0, True), [])

    all_but_one(rs_recv, NX * NY, coll_sem.at[1])
    acc = rs_recv[0].astype(F32)
    for i in range(1, NX * NY):
        acc = acc + rs_recv[i].astype(F32)
    rz_send[...] = acc.astype(BF16)
    rz_recv[z] = rz_send[...]

    for i in LINE:
        remote(
            rz_send,
            rz_recv.at[z],
            coll_sem.at[2],
            coll_sem.at[3],
            z_peer((z + i) % NZ),
        ).start()

    def onward(near):
        for up, k in ((1, 0), (0, 2)):

            @pl.when((zl == up) == near)
            def _():
                got_y_own(up)
                start(inner(3 + k))
                start(to_x(1, k, 0))
                start(to_x(0, k, 0))

    onward(True)
    got_x_middle(0)
    for col in (1, 7):
        start(inner(col))
    onward(False)
    got_x_middle(1)
    got_inner(1)
    weave(radial_steps(1, 0), [])
    weave(radial_steps(7, 1), pool_steps(1, 0))
    got_y_ends()
    for k in (0, 2):
        start(to_x(1, k, 1))
        start(to_x(0, k, 1))
    got_inner(3)
    weave(radial_steps(3, 0), pool_steps(7, 1))
    weave(radial_steps(5, 1), pool_steps(3, 0))
    all_of(bytes_of, load_sem.at[4])
    mix_high = mix_ref[...].astype(BF16)
    mix_low = (mix_ref[...] - mix_high.astype(F32)).astype(BF16)

    all_but_one(rz_recv, NZ, coll_sem.at[3])
    total = rz_recv[0].astype(F32)
    for i in range(1, NZ):
        total = total + rz_recv[i].astype(F32)
    product = filt[...] * (total * (1.0 / 256.0))
    high = product.astype(BF16)
    low = (product - high.astype(F32)).astype(BF16)
    block = (
        jnp.dot(high, mix_high, preferred_element_type=F32)
        + jnp.dot(low, mix_high, preferred_element_type=F32)
        + jnp.dot(high, mix_low, preferred_element_type=F32)
    ).astype(BF16)
    ga_send[...] = block

    for i, j in PLANE:
        back = (4 - i) % 4
        remote(
            ga_send,
            ga_recv.at[back * 4 + (4 - j) % 4],
            coll_sem.at[4],
            ga_sem.at[back],
            plane_peer(i, j)[1],
        ).start()
    ga_recv[0] = block
    corners = ((1, 0, 0), (1, 2, 2), (0, 0, 6), (0, 2, 8))
    for up, k, col in corners:
        got_x(up, k, 0)
        start(inner(col))
    before = pool_steps(5, 1)
    for i, (up, k, col) in enumerate(corners):
        got_x(up, k, 1)
        got_inner(col)
        weave(radial_steps(col, i % 2), before)
        before = pool_steps(col, i % 2)
    weave(before, [])

    for t in range(2):
        message = jnp.zeros((TILE, D), F32)
        for r in range(NRBF):
            weight = math.exp(-18.0 * ((r + 0.5) / NRBF) ** 2)
            pooled = (pool[t, r * TILE : (r + 1) * TILE] * weight).astype(BF16)
            message = message + jnp.dot(
                pooled, rmix_ref[r * D : (r + 1) * D], preferred_element_type=F32
            )
        far[t * TILE : (t + 1) * TILE] = message + halo[17 + t].astype(F32)

    theirs = 0.0
    for i in (0, 1, 3, 2):
        some = ga_recv.at[pl.ds(i * 4, 4 if i else 3)]
        all_of(some, ga_sem.at[i])
        theirs = theirs + jnp.dot(
            tab_i[2 * TILE :, i * 256 : i * 256 + 256],
            ga_recv[i * 4 : i * 4 + 4].reshape(256, D),
            preferred_element_type=F32,
        )
    ls_send[...] = theirs.astype(BF16)
    last = remote(ls_send, ls_recv, coll_sem.at[5], coll_sem.at[6], partner)
    last.start()
    ours = far[...] + jnp.dot(
        tab_i[: 2 * TILE], ga_recv[...].reshape(K, D), preferred_element_type=F32
    )
    last.wait_recv()
    summed = ours + ls_recv[...].astype(F32)
    mean = jnp.mean(summed * summed, axis=-1, keepdims=True)
    normed = summed * lax.rsqrt(mean + EPS) * gain_ref[...]
    hidden = jnp.dot(normed.astype(BF16), up_ref[...], preferred_element_type=F32)
    hidden = hidden / (1.0 + jnp.exp(-hidden))
    updated = summed + jnp.dot(
        hidden.astype(BF16), down_ref[...], preferred_element_type=F32
    )
    out_ref[...] = updated.astype(BF16).reshape(2, TILE, D)

    all_of(halo.at[pl.ds(0, 34)], send_sem.at[0])
    all_of(halo_pos, send_sem.at[1])
    all_of(sx_send, send_sem.at[2])
    all_but_one(rs_send, NX * NY, coll_sem.at[0])
    all_but_one(rz_recv, NZ, coll_sem.at[2])
    all_but_one(ga_recv, NX * NY, coll_sem.at[4])
    all_of(ls_send, coll_sem.at[5])


def on_device(features, positions, waves, rmix, cw, filters, mix, gain, up, down):
    feat = features.reshape(2, TILE, D)
    pos = positions.reshape(3, 2, TILE)
    hbm = pl.BlockSpec(memory_space=pl.ANY)
    dma = pltpu.SemaphoreType.DMA
    vmem = pltpu.VMEM
    out = pl.pallas_call(
        kernel,
        out_shape=pltpu.VMEM((2, TILE, D), BF16),
        in_specs=[hbm] * 10,
        out_specs=pl.BlockSpec(memory_space=pltpu.VMEM),
        scratch_shapes=[
            vmem((3, 2, TILE), jnp.int32),
            vmem((3, K), jnp.int32),
            vmem((D, D), BF16),
            vmem((64, D), F32),
            vmem((D, D), F32),
            vmem((NRBF * D, D), BF16),
            vmem((1, D), F32),
            vmem((D, 2 * D), BF16),
            vmem((2 * D, D), BF16),
            vmem((36, TILE, D), BF16),
            vmem((36, 3, 1, TILE), jnp.int32),
            vmem((2, 3, 1, TILE), jnp.int32),
            vmem((4 * TILE, K), BF16),
            vmem((K, D), BF16),
            vmem((K, D), BF16),
            vmem((K, D), F32),
            vmem((16, 64, D), BF16),
            vmem((16, 64, D), BF16),
            vmem((64, D), BF16),
            vmem((NZ, 64, D), BF16),
            vmem((64, D), BF16),
            vmem((16, 64, D), BF16),
            vmem((2 * TILE, D), BF16),
            vmem((2 * TILE, D), BF16),
            vmem((16, K), F32),
            vmem((K, 16), BF16),
            vmem((4 * TILE, 16), BF16),
            vmem((2 * TILE, D), BF16),
            vmem((2, 2, TILE, 3 * TILE), F32),
            vmem((2, TILE, 16), BF16),
            vmem((NRBF * TILE, 3 * TILE), BF16),
            vmem((NRBF * TILE, 3 * TILE), BF16),
            vmem((NRBF * TILE, 3 * TILE), BF16),
            vmem((NRBF * TILE, 3 * TILE), BF16),
            vmem((2, NRBF * TILE, D), F32),
            vmem((2 * TILE, D), F32),
            vmem((833, 1, D), F32),
            dma((5,)),
            dma((3,)),
            dma,
            dma,
            dma((3,)),
            dma((2, 5)),
            dma((7,)),
            dma,
            dma((7,)),
            dma((4,)),
            pltpu.SemaphoreType.REGULAR,
        ],
        compiler_params=pltpu.CompilerParams(collective_id=0, has_side_effects=True),
    )(feat, pos, waves, cw, filters, mix, rmix, gain.reshape(1, D), up, down)
    return out.reshape(features.shape)


def solution(mesh):
    tiles = P("gx", "gy", "gz", None, None)
    in_specs = (tiles, P(None, "gx", "gy", "gz", None)) + (P(),) * 8
    return jax.shard_map(
        on_device, mesh=mesh, in_specs=in_specs, out_specs=tiles, check_vma=False
    )
```

```python
import functools
import math

import jax
import jax.numpy as jnp
from jax import lax
from jax.experimental import pallas as pl
from jax.experimental.pallas import tpu as pltpu
from jax.sharding import PartitionSpec as P

MESH = pl.DeviceIdType.MESH
F32, BF16 = jnp.float32, jnp.bfloat16
NRBF = 6
GRID = 64
TILE = 128
D = 128
K = 1024
EPS = 1e-06
NX, NY, NZ = 4, 4, 8
LOG2E = 1.4426950408889634
ROUND = 12582912.0
SIN = (
    6.283182818518357,
    -41.341421396050286,
    81.5961838134782,
    -76.58009997779837,
    41.20539265997673,
    -12.271259128462068,
)
ORDER = (2, 1, 3, 0)
ALONG = [(i, j) for i in (2, 1) for j in ORDER]
BACK = [(3, 2), (0, 2), (3, 1), (0, 1), (3, 3), (0, 3), (3, 0)]
PLANE = [step for pair in zip(ALONG, BACK) for step in pair] + ALONG[7:]
INNER = (3, 2, 4, 1, 0, 1, 5, 2, 6)
LINE = sorted(range(1, 8), key=lambda i: -min(i, 8 - i))
FIRST = (((0,), (0,)), ((), ()))


def rows16(values, width):
    row = lax.broadcasted_iota(jnp.int32, (16, width), 0)
    out = jnp.zeros((16, width), F32)
    for at, value in enumerate(values):
        out = jnp.where(row == at, value, out)
    return out


def sine_of_cycles(cycles):
    f = cycles - ((cycles + ROUND) - ROUND)
    u = f * f
    acc = SIN[5]
    for c in SIN[4::-1]:
        acc = acc * u + c
    return acc * f


def lanes(tiles):
    return jnp.concatenate(tiles, axis=1)


def kernel(
    feat_hbm,
    pos_hbm,
    wave_hbm,
    cw_hbm,
    filt_hbm,
    mix_hbm,
    rmix_hbm,
    gain_hbm,
    up_hbm,
    down_hbm,
    out_ref,
    pos_own,
    wave_ref,
    cw_ref,
    filt,
    mix_ref,
    rmix_ref,
    gain_ref,
    up_ref,
    down_ref,
    halo,
    halo_pos,
    pair_pos,
    tab_i,
    sx_send,
    sx_recv,
    s_own,
    rs_send,
    rs_recv,
    rz_send,
    rz_recv,
    ga_send,
    ga_recv,
    ls_send,
    ls_recv,
    kv,
    kt,
    ct,
    charge,
    q2,
    targets,
    rad0,
    rad1,
    rad2,
    rad3,
    pool,
    far,
    bytes_of,
    load_sem,
    send_sem,
    pair_sem,
    hz_sem,
    hy_sem,
    hx_sem,
    hc_sem,
    sx_sem,
    coll_sem,
    ga_sem,
    met_sem,
):
    gx, gy, gz = lax.axis_index("gx"), lax.axis_index("gy"), lax.axis_index("gz")
    y, zl, zh, c = gy // 2, gy % 2, gz // 2, gz % 2
    z = zh * 2 + zl
    q = gx * NY + y

    def at(gx_, gy_, gz_):
        return {"gx": gx_, "gy": gy_, "gz": gz_}

    def turn(i):
        return (4 - i) % 4 * c + i * (1 - c)

    def plane_peer(i, j):
        x_, y_ = (gx + turn(i)) % NX, (y + turn(j)) % NY
        return x_ * NY + y_, at(x_, y_ * 2 + zl, gz)

    def z_peer(i):
        return at(gx, y * 2 + i % 2, (i // 2) * 2 + c)

    partner = at(gx, gy, gz + 1 - 2 * c)
    cross = at(gx, gy, (gz + 2 * c + 7) % 8)
    gy_up, gy_down = at(gx, (gy + 1) % 8, gz), at(gx, (gy + 7) % 8, gz)
    gx_up, gx_down = at((gx + 1) % 4, gy, gz), at((gx + 3) % 4, gy, gz)
    far_y = at(gx, (gy + 2 * zl + 7) % 8, gz)

    barrier = pltpu.get_barrier_semaphore()

    def signal(sem, peer):
        pl.semaphore_signal(sem, inc=1, device_id=peer, device_id_type=MESH)

    def remote(src, dst, send, recv, peer):
        return pltpu.make_async_remote_copy(
            src_ref=src,
            dst_ref=dst,
            send_sem=send,
            recv_sem=recv,
            device_id=peer,
            device_id_type=MESH,
        )

    def all_of(ref, sem):
        pltpu.make_async_copy(ref, ref, sem).wait()

    mine = pl.multiple_of(q * 64, 64)
    pairs = [
        (pos_hbm, pos_own),
        (wave_hbm, wave_ref),
        (feat_hbm, halo.at[pl.ds(17, 2)]),
        (cw_hbm, cw_ref),
        (filt_hbm.at[pl.ds(mine, 64)], filt),
        (mix_hbm, mix_ref),
        (rmix_hbm, rmix_ref),
        (gain_hbm, gain_ref),
        (up_hbm, up_ref),
        (down_hbm, down_ref),
    ]
    loads = [
        pltpu.make_async_copy(src, dst, load_sem.at[min(i, 4)])
        for i, (src, dst) in enumerate(pairs)
    ]
    for load in loads[:4]:
        load.start()

    for load in loads[4:]:
        load.start()

    @pl.when(c == 1)
    def _():
        signal(barrier, partner)
        pl.semaphore_wait(met_sem, 1)
        for i, j in PLANE:
            signal(barrier, plane_peer(i, j)[1])
        for i in LINE:
            signal(barrier, z_peer((z + i) % NZ))
        signal(barrier, far_y)

    @pl.when(c == 0)
    def _():
        pl.semaphore_wait(barrier, 1)
        signal(met_sem, partner)

    for load in loads[:2]:
        load.wait()
    waves = wave_ref[...].astype(F32)
    kx = waves[0:1] * (4.0 / 1024.0)
    ky = waves[1:2] * (2.0 / 1024.0)
    kz = waves[2:3] * (1.0 / 1024.0)
    waves = rows16([kx, ky, kz, kx, ky, kz, 1.0], K)
    kv[...] = waves
    kt[...] = waves.T.astype(BF16)
    quarter = jnp.where(c == 0, 0.25, 0.0)

    def coords(px, py, pz, tile_z, shift):
        offsets = [(v * GRID).astype(F32) for v in (gx, gy, tile_z)]
        return rows16(
            [px.astype(F32), py.astype(F32), pz.astype(F32)] + offsets + [shift], TILE
        )

    for t in range(2):
        for i in range(3):
            halo_pos[17 + t, i] = pos_own[i, t : t + 1]

    def own_coords(shift):
        return [
            coords(*(halo_pos[17 + t, i] for i in range(3)), gz * 2 + t, shift)
            for t in range(2)
        ]

    own = own_coords(quarter)
    own_half = lanes(own).astype(BF16)
    other_half = lanes(own_coords(0.25 - quarter)).astype(BF16)
    for load in loads[2:4]:
        load.wait()
    own_feat = halo[17:19].reshape(2 * TILE, D)
    charge[...] = jnp.dot(own_feat, cw_ref[...], preferred_element_type=F32).astype(BF16)

    def factors(b, atoms):
        rows = pl.ds(pl.multiple_of(b * 128, 128), 128)
        cycles = jnp.dot(kt[rows], atoms, preferred_element_type=F32)
        table = sine_of_cycles(cycles).astype(BF16)
        return rows, jnp.dot(table, charge[...], preferred_element_type=F32)

    def group(i):
        return pl.multiple_of((gx + i) % NX * 256, 256)

    for i in ORDER:
        for h in range(2):
            rows, part = factors(group(i) // 128 + h, other_half)
            sx_send[rows] = part.astype(BF16)
    for i in ORDER:
        rows = pl.ds(group(i), 256)
        remote(
            sx_send.at[rows], sx_recv.at[rows], send_sem.at[2], sx_sem, partner
        ).start()

    for i in ORDER:
        for h in range(2):
            rows, part = factors(group(i) // 128 + h, own_half)
            s_own[rows] = part

    all_of(sx_recv, sx_sem)
    for i in ORDER:
        rows = pl.ds(group(i), 256)
        both = s_own[rows] + sx_recv[rows].astype(F32)
        rs_send[pl.ds(group(i) // 64, 4)] = both.astype(BF16).reshape(4, 64, D)

    @pl.when(c == 1)
    def _():
        pl.semaphore_wait(barrier, 23)
        signal(met_sem, partner)

    @pl.when(c == 0)
    def _():
        pl.semaphore_wait(met_sem, 1)

    for i, j in PLANE:
        block, peer = plane_peer(i, j)
        remote(
            rs_send.at[block], rs_recv.at[q], coll_sem.at[0], coll_sem.at[1], peer
        ).start()

    def tiles(src, dst, n, sem, peer):
        return [
            remote(
                ref.at[pl.ds(src, n)], ref.at[pl.ds(dst, n)], send_sem.at[i], sem, peer
            )
            for i, ref in enumerate((halo, halo_pos))
        ]

    def got_tiles(n, sem):
        all_of(bytes_of.at[pl.ds(0, 67 * n)], sem)

    pair_copy = remote(
        halo_pos.at[pl.ds(17, 2)], pair_pos, send_sem.at[1], pair_sem, partner
    )

    def inner(col):
        return tiles(col * 4 + 2 - c, col * 4 + 3 * c, 1, hc_sem.at[INNER[col]], partner)

    def sides(src, dst, end, sem, peer):
        if end:
            return tiles(src * 4 + 3 * c, dst * 4 + 3 * c, 1, sem, peer)
        return tiles(src * 4 + 1, dst * 4 + 1, 2, sem, peer)

    def to_y(up, end):
        col, peer = (3, gy_up) if up else (5, gy_down)
        return sides(4, col, end, hy_sem.at[2 * end + (0 if end else up)], peer)

    def to_x(up, k, end):
        peer = gx_up if up else gx_down
        dst = (0 if up else 6) + k
        return sides(3 + k, dst, end, hx_sem.at[end, 4 if k == 1 else 2 * up + k // 2], peer)

    def start(copies):
        for copy in copies:
            copy.start()

    def got_y_own(up):
        got_tiles(2, hy_sem.at[up])

    def got_y_ends():
        got_tiles(2, hy_sem.at[2])

    def got_x_middle(end):
        got_tiles(2 * (2 - end), hx_sem.at[end, 4])

    def got_x(up, k, end):
        got_tiles(2 - end, hx_sem.at[end, 2 * up + k // 2])

    def got_inner(col):
        got_tiles(INNER.count(INNER[col]), hc_sem.at[INNER[col]])

    start(tiles(17 + c, 19 - 3 * c, 1, hz_sem, cross))
    pair_copy.start()
    for up in (1, 0):

        @pl.when(zl != up)
        def _():
            start(to_y(up, 0))

    start(inner(4))
    rs_recv[q] = rs_send[q]

    def all_but_one(buffer, n, sem):
        all_of(buffer.at[pl.ds(0, n - 1)], sem)

    def centre_rows(t):
        px = halo_pos[17 + t, 0] - 32
        py = halo_pos[17 + t, 1] - 32
        pz = halo_pos[17 + t, 2] + (GRID * t - 64)
        norm = px * px + py * py + pz * pz
        high = (norm >> 8) << 8
        scale = 1.0 / 64.0
        values = [-2 * px, -2 * py, -2 * pz, high, norm - high]
        values = [v.astype(F32) * scale for v in values]
        return rows16(values + [scale, scale], TILE)

    for t in range(2):
        targets[t] = centre_rows(t).T.astype(BF16)

    def radial_steps(col, slot):
        def squares():
            dx, dy = col // 3 - 1, col % 3 - 1
            at_ = [[halo_pos[col * 4 + s, i] for s in range(4)] for i in range(3)]
            px = lanes(at_[0]) + (dx * GRID - 32)
            py = lanes(at_[1]) + (dy * GRID - 32)
            pz = lanes([at_[2][s] + (GRID * s - 128) for s in range(4)])
            norm = px * px + py * py + pz * pz
            high = (norm >> 8) << 8
            scale = 1.0 / 64.0
            xs, ys, zs, hs, ls = (
                v.astype(F32) * scale for v in (px, py, pz, high, norm - high)
            )
            sources = rows16(
                [xs, ys, zs, scale, scale, hs, ls], 4 * TILE
            ).astype(BF16)
            for t in range(2):
                q2[slot, t] = jnp.dot(
                    targets[t],
                    sources[:, t * TILE : (t + 3) * TILE],
                    preferred_element_type=F32,
                )

        def some(t, part):
            rad = rads[slot * 2 + t]
            raw = q2[slot, t, part * 16 : part * 16 + 16]
            s2 = jnp.clip(raw, 1.0 / 8192.0, 1.0)
            s = s2 * lax.rsqrt(s2)
            rest = 1.0 - s2
            env = jnp.where(raw > 0.0, rest * rest, 0.0)
            step = jnp.exp2(s * (6.0 * LOG2E))
            value = env * jnp.exp2(s * (3.0 * LOG2E) - s2 * (18.0 * LOG2E))
            for r in range(NRBF):
                first = r * TILE + part * 16
                rad[first : first + 16] = value.astype(BF16)
                if r < NRBF - 1:
                    value = value * step

        return [squares] + [
            functools.partial(some, t, part) for t in range(2) for part in range(8)
        ]

    def pool_steps(col, slot, first=False):
        def some(t, r):
            near = halo[col * 4 + t : col * 4 + t + 3].reshape(3 * TILE, D)
            rows = slice(r * TILE, r * TILE + TILE)
            got = jnp.dot(rads[slot * 2 + t][rows], near, preferred_element_type=F32)
            if first:
                pool[t, rows] = got
            else:
                pool[t, rows] += got

        return [functools.partial(some, t, r) for t in range(2) for r in range(NRBF)]

    def weave(one, two):
        done = 0
        for i, step in enumerate(one or [lambda: None]):
            step()
            while done * max(len(one), 1) < (i + 1) * len(two):
                two[done]()
                done += 1

    rads = (rad0, rad1, rad2, rad3)

    pair_copy.wait_recv()
    other = [
        coords(*(pair_pos[t, i] for i in range(3)), (gz + 1 - 2 * c) * 2 + t, quarter)
        for t in range(2)
    ]
    for t, tile in enumerate(own + other):
        ct[t * TILE : (t + 1) * TILE] = tile.T.astype(BF16)

    turned = []
    for i in range(4):
        part = kv[:, pl.ds(group(i), 256)]
        turned.append(pltpu.roll(part, (NY - y) % NY * 64, axis=1).astype(BF16))

    def table_block(b, carry):
        rows = pl.ds(pl.multiple_of(b * 64, 64), 64)
        for part in range(4):
            cols = slice(part * 256, part * 256 + 256)
            cycles = jnp.dot(ct[rows], turned[part], preferred_element_type=F32)
            tab_i[rows, cols] = sine_of_cycles(cycles).astype(BF16)
        return carry

    lax.fori_loop(0, 4, table_block, 0)
    for up in (1, 0):

        @pl.when(zl == up)
        def _():
            start(to_y(up, 0))

    for up in (1, 0):
        start(to_x(up, 1, 0))
    lax.fori_loop(4, 8, table_block, 0)

    got_tiles(1, hz_sem)
    for up in (1, 0):
        start(to_y(up, 1))
        start(to_x(up, 1, 1))

    got_inner(4)
    weave(radial_steps(4, 0), [])
    weave(pool_steps(4, 0, True), [])

    all_but_one(rs_recv, NX * NY, coll_sem.at[1])
    acc = rs_recv[0].astype(F32)
    for i in range(1, NX * NY):
        acc = acc + rs_recv[i].astype(F32)
    rz_send[...] = acc.astype(BF16)
    rz_recv[z] = rz_send[...]

    for i in LINE:
        remote(
            rz_send,
            rz_recv.at[z],
            coll_sem.at[2],
            coll_sem.at[3],
            z_peer((z + i) % NZ),
        ).start()

    def onward(near):
        for up, k in ((1, 0), (0, 2)):

            @pl.when((zl == up) == near)
            def _():
                got_y_own(up)
                start(inner(3 + k))
                start(to_x(1, k, 0))
                start(to_x(0, k, 0))

    onward(True)
    got_x_middle(0)
    for col in (1, 7):
        start(inner(col))
    onward(False)
    got_x_middle(1)
    got_inner(1)
    weave(radial_steps(1, 0), [])
    weave(radial_steps(7, 1), pool_steps(1, 0))
    got_y_ends()
    for k in (0, 2):
        start(to_x(1, k, 1))
        start(to_x(0, k, 1))
    got_inner(3)
    weave(radial_steps(3, 0), pool_steps(7, 1))
    weave(radial_steps(5, 1), pool_steps(3, 0))
    corners = ((1, 0, 0), (1, 2, 2), (0, 0, 6), (0, 2, 8))

    def relay(near):
        for up, k, col in corners:

            @pl.when((zl == 1 - k // 2) == near)
            def _():
                got_x(up, k, 0)
                start(inner(col))

    relay(True)
    all_of(bytes_of, load_sem.at[4])
    mix_high = mix_ref[...].astype(BF16)
    mix_low = (mix_ref[...] - mix_high.astype(F32)).astype(BF16)

    all_but_one(rz_recv, NZ, coll_sem.at[3])
    total = rz_recv[0].astype(F32)
    for i in range(1, NZ):
        total = total + rz_recv[i].astype(F32)
    product = filt[...] * (total * (1.0 / 256.0))
    high = product.astype(BF16)
    low = (product - high.astype(F32)).astype(BF16)
    block = (
        jnp.dot(high, mix_high, preferred_element_type=F32)
        + jnp.dot(low, mix_high, preferred_element_type=F32)
        + jnp.dot(high, mix_low, preferred_element_type=F32)
    ).astype(BF16)
    ga_send[...] = block

    for i, j in PLANE:
        back = (4 - turn(i)) % 4
        remote(
            ga_send,
            ga_recv.at[back * 4 + (4 - turn(j)) % 4],
            coll_sem.at[4],
            ga_sem.at[back],
            plane_peer(i, j)[1],
        ).start()
    ga_recv[0] = block
    relay(False)
    before = pool_steps(5, 1)
    for i, (up, k, col) in enumerate(corners):
        got_x(up, k, 1)
        got_inner(col)
        weave(radial_steps(col, i % 2), before)
        before = pool_steps(col, i % 2)
    weave(before, [])

    for t in range(2):
        message = jnp.zeros((TILE, D), F32)
        for r in range(NRBF):
            weight = math.exp(-18.0 * ((r + 0.5) / NRBF) ** 2)
            pooled = (pool[t, r * TILE : (r + 1) * TILE] * weight).astype(BF16)
            message = message + jnp.dot(
                pooled, rmix_ref[r * D : (r + 1) * D], preferred_element_type=F32
            )
        far[t * TILE : (t + 1) * TILE] = message + halo[17 + t].astype(F32)

    theirs = 0.0
    for i in (0, 1, 3, 2):
        some = ga_recv.at[pl.ds(i * 4, 4 if i else 3)]
        all_of(some, ga_sem.at[i])
        theirs = theirs + jnp.dot(
            tab_i[2 * TILE :, i * 256 : i * 256 + 256],
            ga_recv[i * 4 : i * 4 + 4].reshape(256, D),
            preferred_element_type=F32,
        )
    ls_send[...] = theirs.astype(BF16)
    last = remote(ls_send, ls_recv, coll_sem.at[5], coll_sem.at[6], partner)
    last.start()
    ours = far[...] + jnp.dot(
        tab_i[: 2 * TILE], ga_recv[...].reshape(K, D), preferred_element_type=F32
    )
    last.wait_recv()
    summed = ours + ls_recv[...].astype(F32)
    mean = jnp.mean(summed * summed, axis=-1, keepdims=True)
    normed = summed * lax.rsqrt(mean + EPS) * gain_ref[...]
    hidden = jnp.dot(normed.astype(BF16), up_ref[...], preferred_element_type=F32)
    hidden = hidden / (1.0 + jnp.exp(-hidden))
    updated = summed + jnp.dot(
        hidden.astype(BF16), down_ref[...], preferred_element_type=F32
    )
    out_ref[...] = updated.astype(BF16).reshape(2, TILE, D)

    all_of(halo.at[pl.ds(0, 34)], send_sem.at[0])
    all_of(halo_pos, send_sem.at[1])
    all_of(sx_send, send_sem.at[2])
    all_but_one(rs_send, NX * NY, coll_sem.at[0])
    all_but_one(rz_recv, NZ, coll_sem.at[2])
    all_but_one(ga_recv, NX * NY, coll_sem.at[4])
    all_of(ls_send, coll_sem.at[5])


def on_device(features, positions, waves, rmix, cw, filters, mix, gain, up, down):
    feat = features.reshape(2, TILE, D)
    pos = positions.reshape(3, 2, TILE)
    hbm = pl.BlockSpec(memory_space=pl.ANY)
    dma = pltpu.SemaphoreType.DMA
    vmem = pltpu.VMEM
    out = pl.pallas_call(
        kernel,
        out_shape=pltpu.VMEM((2, TILE, D), BF16),
        in_specs=[hbm] * 10,
        out_specs=pl.BlockSpec(memory_space=pltpu.VMEM),
        scratch_shapes=[
            vmem((3, 2, TILE), jnp.int32),
            vmem((3, K), jnp.int32),
            vmem((D, D), BF16),
            vmem((64, D), F32),
            vmem((D, D), F32),
            vmem((NRBF * D, D), BF16),
            vmem((1, D), F32),
            vmem((D, 2 * D), BF16),
            vmem((2 * D, D), BF16),
            vmem((36, TILE, D), BF16),
            vmem((36, 3, 1, TILE), jnp.int32),
            vmem((2, 3, 1, TILE), jnp.int32),
            vmem((4 * TILE, K), BF16),
            vmem((K, D), BF16),
            vmem((K, D), BF16),
            vmem((K, D), F32),
            vmem((16, 64, D), BF16),
            vmem((16, 64, D), BF16),
            vmem((64, D), BF16),
            vmem((NZ, 64, D), BF16),
            vmem((64, D), BF16),
            vmem((16, 64, D), BF16),
            vmem((2 * TILE, D), BF16),
            vmem((2 * TILE, D), BF16),
            vmem((16, K), F32),
            vmem((K, 16), BF16),
            vmem((4 * TILE, 16), BF16),
            vmem((2 * TILE, D), BF16),
            vmem((2, 2, TILE, 3 * TILE), F32),
            vmem((2, TILE, 16), BF16),
            vmem((NRBF * TILE, 3 * TILE), BF16),
            vmem((NRBF * TILE, 3 * TILE), BF16),
            vmem((NRBF * TILE, 3 * TILE), BF16),
            vmem((NRBF * TILE, 3 * TILE), BF16),
            vmem((2, NRBF * TILE, D), F32),
            vmem((2 * TILE, D), F32),
            vmem((833, 1, D), F32),
            dma((5,)),
            dma((3,)),
            dma,
            dma,
            dma((3,)),
            dma((2, 5)),
            dma((7,)),
            dma,
            dma((7,)),
            dma((4,)),
            pltpu.SemaphoreType.REGULAR,
        ],
        compiler_params=pltpu.CompilerParams(collective_id=0, has_side_effects=True),
    )(feat, pos, waves, cw, filters, mix, rmix, gain.reshape(1, D), up, down)
    return out.reshape(features.shape)


def solution(mesh):
    tiles = P("gx", "gy", "gz", None, None)
    in_specs = (tiles, P(None, "gx", "gy", "gz", None)) + (P(),) * 8
    return jax.shard_map(
        on_device, mesh=mesh, in_specs=in_specs, out_specs=tiles, check_vma=False
    )
```
